128 devices in a mesh: row: 16 (over y_lo, z, core), col: 8 (over x, y_hi).
Axes of the slice: x: 4, y: 4 (y_hi: 2, y_lo: 2; y = y_hi * 2 + y_lo), z: 4, core: 2. Of those that a mesh axis runs over, the one named last changes fastest.
Arguments:
- potential: float32 [512, 512, 512], P(('row', 'col')), may hold values from -6 to 6
- basis_left: bfloat16 [8192, 128, 384], P(('row', 'col')), may hold values from -1.1953125 to 1.1953125
- basis_right: bfloat16 [8192, 128, 384], P(('row', 'col')), may hold values from -1.1953125 to 1.1953125
- core_matrix: bfloat16 [8192, 8192], P('row', 'col'), may hold values from -3 to 3
- density: bfloat16 [8192, 8192], P('row', 'col'), as said below
- pattern: int32 [64, 64], replicated, may hold values from 0 to 1, as said below
- pair_atoms: int32 [8192, 2], P(('row', 'col')), may hold values from 0 to 63, as said below
- cube_offsets: int32 [8192, 3], P(('row', 'col')), may hold values from 0 to 504, as said below
- live_count: int32 [128], P(('row', 'col')), may hold values from 32 to 64, as said below
Outputs:
- hamiltonian: bfloat16 [8192, 8192], P('row', 'col')
- product: float32 [8192, 8192], P('row', 'col')
The draws below stay inside these ranges and needn't reach their ends.
Inputs may be any that keep to these rules, and one draw needn't show every extreme that they name: `pattern`: symmetric; every diagonal block is 1. density is symmetric. `pair_atoms`: the owner of block (i, j) is (i // 4, j // 8) on a 16 x 8 grid. Among the 64 entry slots of one slab at most 1 name blocks of one owner, and in every draw one owner is named by a live entry of every slab. `cube_offsets`: column 0 is at most 2, column 1 at most 504, column 2 at most 504. `live_count`: some slab uses all its slots.
All inputs are finite; a program needn't handle non-finite values.
Results may differ from the reference program's by a relative error of at most 0.0092.
Values may be sent and summed in bfloat16 or wider, within the bound.
A program may use at most 192 MiB of HBM per device.

```python
import math
import jax
import jax.numpy as jnp
from jax import lax

NB = 128
NATOMS = 64
CX = 4
NY = 512
NZ = 512
E_DEV = 64
HALO = 2
CUBE_X = 6
CUBE = 8
CUBE_CELLS = 384
NBAS = 8192
NX = 512
SLOTS = 8192
N_ROW = 16
N_COL = 8


def broad_shift(key):
    return jax.random.randint(jax.random.fold_in(key, 41), (), 0, NATOMS // N_COL).astype(jnp.int32)


def draw_density(key, part):
    order = NATOMS * NB
    base_key = jax.random.fold_in(key, 5)
    base = jax.random.normal(base_key, (order, order), jnp.float32)
    return ((base + base.T) * (0.70710678 / math.sqrt(order))).astype(jnp.bfloat16)


def draw_pattern(key, part):
    col_atoms = NATOMS // N_COL
    reach = jax.random.randint(jax.random.fold_in(key, 3), (NATOMS,), 1, NATOMS // 4 + 1)
    index = jnp.arange(NATOMS, dtype=jnp.int32)
    reach = jnp.where(index % col_atoms == broad_shift(key), NATOMS // 2, reach)
    apart = jnp.abs(index[:, None] - index[None, :])
    apart = jnp.minimum(apart, NATOMS - apart)
    return (apart <= jnp.maximum(reach[:, None], reach[None, :])).astype(jnp.int32)


def draw_pair_atoms(key, part):
    devices = N_ROW * N_COL
    capacity = (E_DEV + devices - 1) // devices
    hot_owner = jax.random.randint(jax.random.fold_in(key, 7), (), 0, devices)
    slab_keys = jax.random.split(jax.random.fold_in(key, 9), devices)

    def slab_order(slab_key):
        others = capacity + jax.random.permutation(slab_key, devices * capacity - capacity)
        joined = jnp.concatenate([jnp.arange(capacity, dtype=jnp.int32), others.astype(jnp.int32)])
        return joined[:E_DEV]
    orders = jax.vmap(slab_order)(slab_keys)
    owners = (orders + hot_owner * capacity) % (devices * capacity) // capacity
    row_atoms = NATOMS // N_ROW
    col_atoms = NATOMS // N_COL
    local_block = jax.random.randint(jax.random.fold_in(key, 11), (devices, E_DEV), 0, row_atoms * col_atoms)
    first_atom = owners // N_COL * row_atoms + local_block // col_atoms
    second_atom = owners % N_COL * col_atoms + local_block % col_atoms
    slot_index = jnp.arange(E_DEV, dtype=jnp.int32)[None, :]
    broad_atom = owners % N_COL * col_atoms + broad_shift(key)
    second_atom = jnp.where(slot_index < 2, broad_atom, second_atom)
    return jnp.stack([first_atom, second_atom], axis=-1).reshape(devices * E_DEV, 2).astype(jnp.int32)


def draw_cube_offsets(key, part):
    total = N_ROW * N_COL * E_DEV
    top_x = CX + 2 * HALO - CUBE_X
    slot_index = jnp.arange(total, dtype=jnp.int32) % E_DEV
    along_x = jax.random.randint(jax.random.fold_in(key, 19), (total,), 0, top_x + 1)
    along_x = jnp.where(slot_index == 0, 0, jnp.where(slot_index == 1, top_x, along_x))
    along_y = jax.random.randint(jax.random.fold_in(key, 23), (total,), 0, NY - CUBE + 1)
    along_z = jax.random.randint(jax.random.fold_in(key, 29), (total,), 0, NZ - CUBE + 1)
    return jnp.stack([along_x, along_y, along_z], axis=-1).astype(jnp.int32)


def draw_live_count(key, part):
    devices = N_ROW * N_COL
    counts = jax.random.randint(jax.random.fold_in(key, 13), (devices,), E_DEV // 2, E_DEV + 1)
    fullest = jax.random.randint(jax.random.fold_in(key, 17), (), 0, devices)
    return jnp.where(jnp.arange(devices) == fullest, E_DEV, counts).astype(jnp.int32)


def shard_levels(key, dims, cuts, smallest, largest):
    factor_of = 1.0
    for axis_at, parts in cuts:
        heights = jax.random.uniform(jax.random.fold_in(jax.random.fold_in(key, 6), axis_at), (parts,), jnp.float32, smallest / len(cuts), largest / len(cuts))
        factor_of = factor_of * jnp.repeat(jnp.exp(heights), dims[axis_at] // parts).reshape((-1,) + (1,) * (len(dims) - 1 - axis_at))
    return factor_of


def bell_draw(stream_key, shape, deviation, bound, cuts=(), kind=jnp.bfloat16):
    entries = deviation * jax.random.normal(stream_key, shape, jnp.float32)
    if cuts:
        entries = entries * shard_levels(stream_key, shape, cuts, -0.22, 0.18)
    return jnp.clip(entries, -bound, bound).astype(kind)


def setup_inputs(seed: int = 0) -> dict:
    key_list = jax.random.split(jax.random.key(seed), 10)
    return {
        "potential": bell_draw(key_list[0], (NX, NY, NZ), 1.0, 6.0, ((0, 128),), jnp.float32),
        "basis_left": bell_draw(key_list[1], (SLOTS, NB, CUBE_CELLS), 0.2, 1.1953125, ((0, 128),)),
        "basis_right": bell_draw(key_list[2], (SLOTS, NB, CUBE_CELLS), 0.2, 1.1953125, ((0, 128),)),
        "core_matrix": bell_draw(key_list[3], (NBAS, NBAS), 0.5, 3.0, ((0, 16), (1, 8))),
        "density": draw_density(jax.random.fold_in(key_list[9], 71), 0),
        "pattern": draw_pattern(jax.random.fold_in(key_list[9], 71), 0),
        "pair_atoms": draw_pair_atoms(jax.random.fold_in(key_list[9], 71), 0),
        "cube_offsets": draw_cube_offsets(jax.random.fold_in(key_list[9], 71), 0),
        "live_count": draw_live_count(jax.random.fold_in(key_list[9], 71), 0),
    }


HIGHEST = lax.Precision.HIGHEST


def block_mask(values, pattern_tile, block_size):
    row_blocks, col_blocks = pattern_tile.shape
    shaped = values.reshape(row_blocks, block_size, col_blocks, block_size)
    selected = (pattern_tile > 0)[:, None, :, None]
    kept = jnp.where(selected, shaped, jnp.zeros((), values.dtype))
    return kept.reshape(row_blocks * block_size, col_blocks * block_size)


def reference(potential, basis_left, basis_right, core_matrix, density, pattern, pair_atoms, cube_offsets, live_count):
    devices = N_ROW * N_COL
    slab_planes = NX // devices
    slot_total = pair_atoms.shape[0]
    per_slab = slot_total // devices
    ordinal = jnp.arange(slot_total, dtype=jnp.int32)
    slab_index = ordinal // per_slab
    live_flag = ((ordinal % per_slab) < live_count[slab_index]).astype(jnp.float32)

    def integrate(entry):
        left_table, right_table, offsets, slab_number, flag_value = entry
        planes = (slab_number * slab_planes - HALO + offsets[0] + jnp.arange(CUBE_X, dtype=jnp.int32)) % NX
        slab_rows = jnp.take(potential, planes.astype(jnp.int32), axis=0)
        start = (jnp.zeros((), jnp.int32), offsets[1].astype(jnp.int32), offsets[2].astype(jnp.int32))
        cube_cells = lax.dynamic_slice(slab_rows, start, (CUBE_X, CUBE, CUBE)).reshape(-1)
        weighted = (left_table.astype(jnp.float32) * cube_cells[None, :]).astype(jnp.bfloat16)
        block_value = jnp.dot(weighted.astype(jnp.float32), right_table.astype(jnp.float32).T, precision=HIGHEST)
        return block_value * flag_value

    partials = lax.map(integrate, (basis_left, basis_right, cube_offsets, slab_index, live_flag))
    block_id = (pair_atoms[:, 0] * NATOMS + pair_atoms[:, 1]).astype(jnp.int32)
    summed = jax.ops.segment_sum(partials, block_id, num_segments=NATOMS * NATOMS)
    integrals = summed.reshape(NATOMS, NATOMS, NB, NB).transpose(0, 2, 1, 3).reshape(NATOMS * NB, NATOMS * NB)
    hamiltonian = block_mask(core_matrix.astype(jnp.float32) + integrals, pattern, NB).astype(jnp.bfloat16)
    masked_density = block_mask(density, pattern, NB)
    product = jnp.dot(hamiltonian.astype(jnp.float32), masked_density.astype(jnp.float32), precision=HIGHEST)
    return hamiltonian, product
```

```python
import functools

import jax
import jax.numpy as jnp
from jax import lax
from jax.experimental import pallas as pl
from jax.experimental.pallas import tpu as pltpu
from jax.sharding import PartitionSpec as P

NATOMS = 64
NB = 128
CELLS = 384
ROWS = 16
COLS = 8
DEVICES = 128
ENTRIES = 64
ATOM_ROWS = 4
ATOM_COLS = 8
LOCAL = ATOM_ROWS * ATOM_COLS
TILE_R = 512
TILE_C = 1024
HALF = 256
MESH = pl.DeviceIdType.MESH
F32 = jnp.float32
BF16 = jnp.bfloat16
I32 = jnp.int32


def vmem():
    return pl.BlockSpec(memory_space=pltpu.VMEM)


def smem():
    return pl.BlockSpec(memory_space=pltpu.SMEM)


def hbm():
    return pl.BlockSpec(memory_space=pl.ANY)


def cube_kernel(
    own_off, left_off, right_off, pairs, live, pattern, corner, pot, density,
    own_out, right_out, left_out, entry_of, ids, masked, windows,
):
    lane = lax.broadcasted_iota(I32, (8, 128), 1)
    line = lax.broadcasted_iota(I32, (8, 128), 0)

    def cut(e, carry):
        for section, (off, first) in enumerate(
            ((own_off, 0), (own_off, 2), (right_off, 2), (left_off, 0))
        ):
            y = off[e, 1]
            z = off[e, 2]
            drop = y % 8
            turn = z % 128
            top = pl.multiple_of(y // 8 * 8, 8)
            below = pl.multiple_of(jnp.minimum(y // 8 + 1, 63) * 8, 8)
            near = pl.multiple_of(z // 128 * 128, 128)
            far = pl.multiple_of(jnp.minimum(z // 128 + 1, 3) * 128, 128)
            for p in range(2):
                quarter = [
                    [pot[first + p, pl.ds(r, 8), pl.ds(c, 128)] for c in (near, far)]
                    for r in (top, below)
                ]
                upper, lower = [jnp.where(lane >= turn, a, b) for a, b in quarter]
                window = jnp.where(line >= drop, upper, lower)
                window = pltpu.roll(window, (8 - drop) % 8, 0)
                window = pltpu.roll(window, (128 - turn) % 128, 1)
                start = pl.multiple_of(e * 16 + p * 8, 8)
                windows[section, pl.ds(start, 8), :] = window
        return carry

    lax.fori_loop(0, ENTRIES, cut, 0)

    def clear(d, carry):
        entry_of[d] = 0
        return carry

    lax.fori_loop(0, DEVICES, clear, 0)
    ids[...] = jnp.full(ids.shape, -1, I32)

    def place(e, carry):
        @pl.when(e < live[0])
        def _():
            i = pairs[e, 0]
            j = pairs[e, 1]
            owner = i // ATOM_ROWS * COLS + j // ATOM_COLS
            entry_of[owner] = e
            ids[owner] = jnp.full((1, 128), i % ATOM_ROWS * ATOM_COLS + j % ATOM_COLS, I32)

        return carry

    lax.fori_loop(0, ENTRIES, place, 0)

    rows = ENTRIES * 16
    at = lax.broadcasted_iota(I32, (128, 128), 0)
    to = lax.broadcasted_iota(I32, (128, 128), 1)
    spread = jnp.where(at == to % 8, 1.0, 0.0).astype(BF16)
    r = lax.broadcasted_iota(I32, (rows, 128), 0)
    c = lax.broadcasted_iota(I32, (rows, 128), 1)
    keep = (r % 16) == c // 8
    fold = jnp.where(
        lax.broadcasted_iota(I32, (ENTRIES, rows), 1) // 16
        == lax.broadcasted_iota(I32, (ENTRIES, rows), 0),
        1.0,
        0.0,
    ).astype(BF16)
    for section in range(4):
        wide = jnp.dot(windows[section].astype(BF16), spread, preferred_element_type=F32)
        wide = jnp.where(keep, wide, 0.0).astype(BF16)
        piece = jnp.dot(fold, wide, preferred_element_type=F32).astype(BF16)
        if section == 0:
            own_out[:, 0:128] = piece
        elif section == 1:
            own_out[:, 128:256] = piece
        elif section == 2:
            right_out[...] = piece
        else:
            left_out[...] = piece

    for i in range(ATOM_ROWS):
        for j in range(ATOM_COLS):
            on = pattern[corner[0] + i, corner[1] + j] > 0
            box = (slice(i * NB, (i + 1) * NB), slice(j * NB, (j + 1) * NB))

            @pl.when(on)
            def _():
                masked[box] = density[box]

            @pl.when(jnp.logical_not(on))
            def _():
                masked[box] = jnp.zeros((NB, NB), BF16)


def cut_cubes(own_off, left_off, right_off, pairs, live, pattern, corner, pot, density):
    return pl.pallas_call(
        cube_kernel,
        name="cut_cubes",
        out_shape=(
            jax.ShapeDtypeStruct((ENTRIES, 256), BF16),
            jax.ShapeDtypeStruct((ENTRIES, 128), BF16),
            jax.ShapeDtypeStruct((ENTRIES, 128), BF16),
            jax.ShapeDtypeStruct((DEVICES,), I32),
            jax.ShapeDtypeStruct((DEVICES, 1, 128), I32),
            jax.ShapeDtypeStruct((TILE_R, TILE_C), BF16),
        ),
        in_specs=[smem()] * 7 + [vmem()] * 2,
        out_specs=(vmem(), vmem(), vmem(), smem(), vmem(), vmem()),
        scratch_shapes=[pltpu.VMEM((4, ENTRIES * 16, 128), F32)],
        compiler_params=pltpu.CompilerParams(vmem_limit_bytes=48 << 20),
    )(own_off, left_off, right_off, pairs, live, pattern, corner, pot, density)


def place_of(index):
    return (index // COLS, index % COLS)


def exchange_kernel(
    entry_of, offx, own, to_right, to_left, ids, left, right,
    received, received_ids,
    left_v, right_v, low, high, cubes, blocks, table_sem, near_send, near_recv, send, recv, id_send, id_recv, local,
):
    me = lax.axis_index("row") * COLS + lax.axis_index("col")
    tables = (
        pltpu.make_async_copy(left, left_v, table_sem.at[0]),
        pltpu.make_async_copy(right, right_v, table_sem.at[1]),
    )
    for copy in tables:
        copy.start()
    near = (
        pltpu.make_async_remote_copy(
            to_right, low, near_send.at[0], near_recv.at[0], place_of((me + 1) % DEVICES), MESH
        ),
        pltpu.make_async_remote_copy(
            to_left, high, near_send.at[1], near_recv.at[1], place_of((me + DEVICES - 1) % DEVICES), MESH
        ),
    )
    for copy in near:
        copy.start()

    def id_copy(target):
        return pltpu.make_async_remote_copy(
            ids.at[target], received_ids.at[me], id_send, id_recv, place_of(target), MESH
        )

    def block_copy(target):
        return pltpu.make_async_remote_copy(
            blocks.at[target], received.at[me], send, recv, place_of(target), MESH
        )

    def send_id(k, carry):
        id_copy((me + k) % DEVICES).start()
        return carry

    lax.fori_loop(1, DEVICES, send_id, 0)
    own_id = pltpu.make_async_copy(ids.at[me], received_ids.at[me], local.at[0])
    own_id.start()
    for copy in near:
        copy.wait()
    line = jnp.concatenate([low[...], own[...], high[...]], axis=1).astype(F32)
    at = offx[...]
    cubes[...] = jnp.where(
        at == 0, line[:, 0:384], jnp.where(at == 1, line[:, 64:448], line[:, 128:512])
    )
    for copy in tables:
        copy.wait()

    def make(target):
        e = entry_of[target]
        weighted = left_v[e] * cubes[pl.ds(e, 1), :].astype(BF16)
        block = lax.dot_general(
            weighted, right_v[e], (((1,), (1,)), ((), ())), preferred_element_type=F32
        )
        blocks[target] = block.astype(BF16)

    make(me)
    make((me + 1) % DEVICES)

    def step(k, carry):
        make((me + k) % DEVICES)
        block_copy((me + k - 1) % DEVICES).start()
        return carry

    lax.fori_loop(2, DEVICES, step, 0)
    own_block = pltpu.make_async_copy(blocks.at[me], received.at[me], local.at[1])
    own_block.start()
    block_copy((me + DEVICES - 1) % DEVICES).start()
    own_id.wait()
    own_block.wait()
    all_but_one = pl.ds(0, DEVICES - 1)
    ids_done = pltpu.make_async_remote_copy(
        ids.at[all_but_one], received_ids.at[all_but_one], id_send, id_recv,
        place_of((me + 1) % DEVICES), MESH,
    )
    blocks_done = pltpu.make_async_remote_copy(
        blocks.at[all_but_one], received.at[all_but_one], send, recv,
        place_of((me + 1) % DEVICES), MESH,
    )
    ids_done.wait()
    blocks_done.wait()


def exchange(entry_of, offx, own, to_right, to_left, ids, left, right):
    return pl.pallas_call(
        exchange_kernel,
        name="exchange",
        out_shape=(
            jax.ShapeDtypeStruct((DEVICES, NB, NB), BF16),
            jax.ShapeDtypeStruct((DEVICES, 1, 128), I32),
        ),
        in_specs=[smem()] + [vmem()] * 5 + [hbm()] * 2,
        out_specs=(hbm(), hbm()),
        scratch_shapes=[
            pltpu.VMEM((ENTRIES, NB, CELLS), BF16),
            pltpu.VMEM((ENTRIES, NB, CELLS), BF16),
            pltpu.VMEM((ENTRIES, 128), BF16),
            pltpu.VMEM((ENTRIES, 128), BF16),
            pltpu.VMEM((ENTRIES, CELLS), F32),
            pltpu.VMEM((DEVICES, NB, NB), BF16),
            pltpu.SemaphoreType.DMA((2,)),
            pltpu.SemaphoreType.DMA((2,)),
            pltpu.SemaphoreType.DMA((2,)),
            pltpu.SemaphoreType.DMA,
            pltpu.SemaphoreType.DMA,
            pltpu.SemaphoreType.DMA,
            pltpu.SemaphoreType.DMA,
            pltpu.SemaphoreType.DMA((2,)),
        ],
        compiler_params=pltpu.CompilerParams(
            has_side_effects=True, vmem_limit_bytes=48 << 20
        ),
    )(entry_of, offx, own, to_right, to_left, ids, left, right)


def combine_kernel(pattern, corner, ids_hbm, received, core, ham, total, ids, sem):
    copy = pltpu.make_async_copy(ids_hbm, ids, sem)
    copy.start()
    total[...] = jnp.zeros(total.shape, F32)
    copy.wait()

    def add(s, carry):
        slot = ids[s, 0, 0]

        @pl.when(slot >= 0)
        def _():
            total[slot] += received[s].astype(F32)

        return carry

    lax.fori_loop(0, DEVICES, add, 0)
    for i in range(ATOM_ROWS):
        for j in range(ATOM_COLS):
            on = pattern[corner[0] + i, corner[1] + j] > 0
            box = (slice(i * NB, (i + 1) * NB), slice(j * NB, (j + 1) * NB))

            @pl.when(on)
            def _():
                ham[box] = (core[box].astype(F32) + total[i * ATOM_COLS + j]).astype(BF16)

            @pl.when(jnp.logical_not(on))
            def _():
                ham[box] = jnp.zeros((NB, NB), BF16)


def combine(pattern, corner, ids, received, core):
    return pl.pallas_call(
        combine_kernel,
        name="combine",
        out_shape=jax.ShapeDtypeStruct((TILE_R, TILE_C), BF16),
        in_specs=[smem(), smem(), hbm(), vmem(), vmem()],
        out_specs=vmem(),
        scratch_shapes=[
            pltpu.VMEM((LOCAL, NB, NB), F32),
            pltpu.SMEM((DEVICES, 1, 128), I32),
            pltpu.SemaphoreType.DMA,
        ],
        compiler_params=pltpu.CompilerParams(vmem_limit_bytes=48 << 20),
    )(pattern, corner, ids, received, core)


def product_kernel(ham, den, out, hbuf, dbuf, load, hsend, dsend, csend, hrecv, drecv):
    row = lax.axis_index("row")
    col = lax.axis_index("col")
    core = row % 2
    z = row // 2 % 4
    ylo = row // 8
    x = col // 2
    yhi = col % 2

    def col_of(x_, h_):
        return x_ % 4 * 2 + h_

    def row_of(l_, z_, c_):
        return l_ * 8 + z_ % 4 * 2 + c_

    def h_at(c, half):
        return hbuf.at[c, pl.ds(half * HALF, HALF), :]

    def d_at(r, half):
        start = pl.multiple_of(r % 2 * TILE_R + half * HALF, HALF)
        return dbuf.at[r // 2, pl.ds(start, HALF), :]

    sent = []

    def h_copy(c, half, target, sem):
        return pltpu.make_async_remote_copy(
            h_at(c, half), h_at(c, half), sem, hrecv.at[c, half], (row, target), MESH
        )

    def d_copy(r, half, target, sem):
        return pltpu.make_async_remote_copy(
            d_at(r, half), d_at(r, half), sem, drecv.at[r, half], (target, col), MESH
        )

    count = {"h": 0, "d": 0, "c": 0}

    def push(kind, make, block, half, target):
        sems = {"h": hsend, "d": dsend, "c": csend}[kind]
        copy = make(block, half, target, sems.at[count[kind]])
        count[kind] += 1
        copy.start()
        sent.append(copy)

    def h_wait(c, half):
        h_copy(c, half, col, hsend.at[0]).wait_recv()

    def d_wait(r, half):
        d_copy(r, half, row, dsend.at[0]).wait_recv()

    first = (
        pltpu.make_async_copy(ham, hbuf.at[col], load.at[0]),
        pltpu.make_async_copy(
            den, dbuf.at[row // 2, pl.ds(pl.multiple_of(core * TILE_R, TILE_R), TILE_R), :], load.at[1]
        ),
    )
    for copy in first:
        copy.start()
    for copy in first:
        copy.wait()

    other_core = row_of(ylo, z, 1 - core)
    h_partner = col_of(x, 1 - yhi)
    d_partner = row_of(1 - ylo, z, core)
    x_up, x_down = col_of(x + 1, yhi), col_of(x + 3, yhi)
    z_up, z_down = row_of(ylo, z + 1, core), row_of(ylo, z + 3, core)

    def h_ring(h_):
        me_ = col_of(x, h_)
        for n in range(2):
            push("h", h_copy, me_, n, x_up)
            push("h", h_copy, me_, 1 - n, x_down)

    def d_ring(l_):
        me_ = row_of(l_, z, core)
        for n in range(2):
            push("d", d_copy, me_, n, z_up)
            push("d", d_copy, me_, 1 - n, z_down)

    def share(r, half):
        push("c", d_copy, r, half, other_core)

    def h_forward(h_):
        h_wait(col_of(x + 3, h_), 0)
        push("h", h_copy, col_of(x + 3, h_), 0, x_up)
        h_wait(col_of(x + 1, h_), 1)
        push("h", h_copy, col_of(x + 1, h_), 1, x_down)

    def d_forward(l_):
        down, up = row_of(l_, z + 3, core), row_of(l_, z + 1, core)
        d_wait(down, 0)
        push("d", d_copy, down, 0, z_up)
        d_wait(up, 1)
        push("d", d_copy, up, 1, z_down)
        share(down, 0)
        share(up, 1)

    def h_rest(h_):
        h_wait(col_of(x + 3, h_), 1)
        h_wait(col_of(x + 1, h_), 0)

    def h_far(h_):
        h_wait(col_of(x + 2, h_), 0)
        h_wait(col_of(x + 2, h_), 1)

    def d_rest(l_):
        down, up = row_of(l_, z + 3, core), row_of(l_, z + 1, core)
        d_wait(down, 1)
        d_wait(up, 0)
        share(down, 1)
        share(up, 0)

    def d_far(l_):
        far = row_of(l_, z + 2, core)
        for n in range(2):
            d_wait(far, n)
            share(far, n)

    def d_other(l_, z_):
        r = row_of(l_, z_, 1 - core)
        for n in range(2):
            d_wait(r, n)

    def multiply(l_, z_, start):
        k = l_ * 4 + z_

        def tile(n, carry):
            columns = pl.ds(pl.multiple_of(n * 256, 256), 256)
            part = jnp.dot(hbuf[k], dbuf[k, :, columns], preferred_element_type=F32)
            if start:
                out[:, columns] = part
            else:
                out[:, columns] += part
            return carry

        lax.fori_loop(0, TILE_C // 256, tile, 0)

    h_ring(yhi)
    for n in range(2):
        push("h", h_copy, col, n, h_partner)
    d_ring(ylo)
    for n in range(2):
        push("d", d_copy, row, n, d_partner)
    for n in range(2):
        share(row, n)

    h_forward(yhi)
    d_forward(ylo)
    for n in range(2):
        h_wait(h_partner, n)
    h_ring(1 - yhi)
    for n in range(2):
        d_wait(d_partner, n)
    d_ring(1 - ylo)
    for n in range(2):
        share(d_partner, n)
    h_rest(yhi)
    d_rest(ylo)
    h_far(yhi)
    d_far(ylo)
    for n in range(4):
        d_other(ylo, z + n)
    multiply(ylo, yhi, True)
    multiply(ylo, 2 + yhi, False)
    h_forward(1 - yhi)
    d_forward(1 - ylo)
    h_rest(1 - yhi)
    d_rest(1 - ylo)
    h_far(1 - yhi)
    multiply(ylo, 1 - yhi, False)
    multiply(ylo, 3 - yhi, False)
    d_far(1 - ylo)
    for n in range(4):
        d_other(1 - ylo, z + n)
    for n in range(4):
        multiply(1 - ylo, n, False)
    for copy in sent:
        copy.wait_send()


def multiply_all(ham, den):
    return pl.pallas_call(
        product_kernel,
        name="product",
        out_shape=jax.ShapeDtypeStruct((TILE_R, TILE_C), F32),
        in_specs=[hbm(), hbm()],
        out_specs=vmem(),
        scratch_shapes=[
            pltpu.VMEM((COLS, TILE_R, TILE_C), BF16),
            pltpu.VMEM((COLS, 2 * TILE_R, TILE_C), BF16),
            pltpu.SemaphoreType.DMA((2,)),
            pltpu.SemaphoreType.DMA((16,)),
            pltpu.SemaphoreType.DMA((16,)),
            pltpu.SemaphoreType.DMA((16,)),
            pltpu.SemaphoreType.DMA((COLS, 2)),
            pltpu.SemaphoreType.DMA((ROWS, 2)),
        ],
        compiler_params=pltpu.CompilerParams(
            has_side_effects=True, vmem_limit_bytes=56 << 20
        ),
    )(ham, den)


def shards(
    potential, basis_left, basis_right, core_matrix, density, pattern, pair_atoms, cube_offsets, live_count
):
    up = [(i, (i + 1) % DEVICES) for i in range(DEVICES)]
    left_off = lax.ppermute(cube_offsets, ("row", "col"), up)
    right_off = lax.ppermute(cube_offsets, ("row", "col"), [(b, a) for a, b in up])
    corner = jnp.stack([lax.axis_index("row") * ATOM_ROWS, lax.axis_index("col") * ATOM_COLS]).astype(I32)
    own, to_right, to_left, entry_of, ids, masked = cut_cubes(
        cube_offsets, left_off, right_off, pair_atoms, live_count, pattern, corner, potential, density
    )
    received, received_ids = exchange(
        entry_of, cube_offsets[:, 0:1], own, to_right, to_left, ids, basis_left, basis_right
    )
    ham = combine(pattern, corner, received_ids, received, core_matrix)
    return ham, multiply_all(ham, masked)


def solution(mesh):
    flat = ("row", "col")
    tile = P("row", "col")
    placed = (
        P(flat, None, None),
        P(flat, None, None),
        P(flat, None, None),
        tile,
        tile,
        P(),
        P(flat, None),
        P(flat, None),
        P(flat),
    )
    return jax.shard_map(
        shards, mesh=mesh, in_specs=placed, out_specs=(tile, tile), check_vma=False
    )
```

```python
import functools

import jax
import jax.numpy as jnp
from jax import lax
from jax.experimental import pallas as pl
from jax.experimental.pallas import tpu as pltpu
from jax.sharding import PartitionSpec as P

NATOMS = 64
NB = 128
CELLS = 384
ROWS = 16
COLS = 8
DEVICES = 128
ENTRIES = 64
ATOM_ROWS = 4
ATOM_COLS = 8
LOCAL = ATOM_ROWS * ATOM_COLS
TILE_R = 512
TILE_C = 1024
HALF = 256
STRIDE = 51
SPLIT = 40
MESH = pl.DeviceIdType.MESH
F32 = jnp.float32
BF16 = jnp.bfloat16
I32 = jnp.int32


def vmem():
    return pl.BlockSpec(memory_space=pltpu.VMEM)


def smem():
    return pl.BlockSpec(memory_space=pltpu.SMEM)


def hbm():
    return pl.BlockSpec(memory_space=pl.ANY)


def place_of(index):
    return (index // COLS, index % COLS)


def exchange_kernel(
    offsets, pairs, live, pattern, pot, density, left, right,
    received, received_ids, near_den,
    pot_v, den_v, left_v, right_v, windows, own_off, other_off, off_s, table, table_s, ids,
    to_right, to_left, low, high, cubes, blocks,
    load_sem, off_send, off_recv, copy_sem, near_send, near_recv, send, recv, id_send, id_recv,
    den_send, den_recv, local,
):
    row = lax.axis_index("row")
    col = lax.axis_index("col")
    me = row * COLS + col
    above = place_of((me + 1) % DEVICES)
    below = place_of((me + DEVICES - 1) % DEVICES)

    loads = [
        pltpu.make_async_copy(a, b, load_sem.at[n])
        for n, (a, b) in enumerate(((density, den_v), (left, left_v), (right, right_v)))
    ]
    pot_loads = [
        pltpu.make_async_copy(
            pot.at[:, :, :, pl.ds(n * 128, 128)], pot_v.at[n], load_sem.at[n + 3]
        )
        for n in range(4)
    ]
    for copy in loads[:1] + pot_loads + loads[1:]:
        copy.start()
    barrier = pltpu.get_barrier_semaphore()

    def greet(k, carry):
        pl.semaphore_signal(
            barrier, inc=1, device_id=place_of((me + k) % DEVICES), device_id_type=MESH
        )
        return carry

    lax.fori_loop(1, DEVICES, greet, 0)

    own_off[...] = jnp.zeros((8, 128), I32)
    own_off[0:1, 0:ENTRIES] = offsets[0:1, :]
    own_y = offsets[1:2, :]
    own_z = offsets[2:3, :]
    for n, value in enumerate(
        (
            own_y >> 3,
            jnp.minimum((own_y >> 3) + 1, 63),
            own_z >> 7,
            jnp.minimum((own_z >> 7) + 1, 3),
            own_y & 7,
            own_z & 127,
        )
    ):
        own_off[n + 1 : n + 2, 0:ENTRIES] = value
    own_scalars = pltpu.make_async_copy(own_off, off_s.at[0], copy_sem.at[0])
    own_scalars.start()

    entry = lax.broadcasted_iota(I32, (ENTRIES, ENTRIES), 0)
    eye = entry == lax.broadcasted_iota(I32, (ENTRIES, ENTRIES), 1)

    def upright(line):
        return jnp.sum(jnp.where(eye, line, 0), axis=1, keepdims=True)

    first = pairs[0:1, :]
    second = pairs[1:2, :]
    owner = upright(first // ATOM_ROWS * COLS + second // ATOM_COLS)
    place = upright(first % ATOM_ROWS * ATOM_COLS + second % ATOM_COLS)
    at_x = upright(offsets[0:1, :])
    ordinal = lax.broadcasted_iota(I32, (ENTRIES, DEVICES), 0)
    target_of = lax.broadcasted_iota(I32, (ENTRIES, DEVICES), 1)
    named = jnp.logical_and(owner == target_of, ordinal < live[0])
    table[...] = jnp.zeros((8, 128), I32)
    table[0:1, :] = jnp.sum(jnp.where(named, ordinal, 0), axis=0, keepdims=True)
    table[1:2, :] = jnp.sum(jnp.where(named, place + 1, 0), axis=0, keepdims=True) - 1
    table_scalars = pltpu.make_async_copy(table, table_s, copy_sem.at[1])
    table_scalars.start()

    loads[0].wait()
    for i in range(ATOM_ROWS):
        for j in range(ATOM_COLS):
            on = jnp.full((NB, NB), pattern[row * ATOM_ROWS + i, col * ATOM_COLS + j], I32) > 0
            box = (slice(i * NB, (i + 1) * NB), slice(j * NB, (j + 1) * NB))
            den_v[box] = jnp.where(on, den_v[box].astype(F32), 0.0).astype(BF16)
    keep_den = pltpu.make_async_copy(den_v, near_den.at[0], local.at[2])
    keep_den.start()

    lane = lax.broadcasted_iota(I32, (8, 128), 1)
    line = lax.broadcasted_iota(I32, (8, 128), 0)

    def cut(source, e, planes):
        y_tiles = (off_s[source, 1, e], off_s[source, 2, e])
        z_tiles = (off_s[source, 3, e], off_s[source, 4, e])
        drop = off_s[source, 5, e]
        turn = off_s[source, 6, e]
        kept = ((lane - turn) & 127) < 8
        for section, plane in planes:
            for p in range(2):
                quarter = [
                    [pot_v[zt, plane + p, yt] for zt in z_tiles] for yt in y_tiles
                ]
                upper, lower = [jnp.where(lane >= turn, a, b) for a, b in quarter]
                window = jnp.where(jnp.logical_and(line >= drop, kept), upper, 0.0)
                window = jnp.where(jnp.logical_and(line < drop, kept), lower, window)
                start = pl.multiple_of(e * 16 + p * 8, 8)
                windows[section, pl.ds(start, 8), :] = window

    def cut_own(e, carry):
        for n in range(4):
            cut(0, e * 4 + n, ((0, 0), (1, 2)))
        return carry

    def cut_others(e, carry):
        for n in range(4):
            cut(1, e * 4 + n, ((2, 2),))
            cut(2, e * 4 + n, ((3, 0),))
        return carry

    pl.semaphore_wait(barrier, DEVICES - 1)
    off_copies = (
        pltpu.make_async_remote_copy(
            own_off, other_off.at[0], off_send.at[0], off_recv.at[0], below, MESH
        ),
        pltpu.make_async_remote_copy(
            own_off, other_off.at[1], off_send.at[1], off_recv.at[1], above, MESH
        ),
    )
    for copy in off_copies:
        copy.start()

    def den_copy(slot, half, device):
        part = pl.ds(half * HALF, HALF)
        return pltpu.make_async_remote_copy(
            den_v.at[part, :], near_den.at[slot, part, :],
            den_send.at[slot, half], den_recv.at[slot, half], device, MESH,
        )

    z = row // 2 % 4
    base = row - z * 2
    den_targets = (
        (1, ((row + 8) % ROWS, col)),
        (2, (base + (z + 1) % 4 * 2, col)),
        (3, (base + (z + 3) % 4 * 2, col)),
    )
    den_copies = [[den_copy(slot, half, device) for slot, device in den_targets] for half in range(2)]
    for copy in den_copies[0]:
        copy.start()

    own_scalars.wait()
    for copy in pot_loads:
        copy.wait()
    lax.fori_loop(0, ENTRIES // 4, cut_own, 0)

    at = lax.broadcasted_iota(I32, (128, 128), 0)
    to = lax.broadcasted_iota(I32, (128, 128), 1)
    spread = jnp.where(at % 8 == to % 8, 1.0, 0.0).astype(BF16)
    rows = ENTRIES * 16
    at_row = lax.broadcasted_iota(I32, (rows, 128), 0)
    at_lane = lax.broadcasted_iota(I32, (rows, 128), 1)
    right_plane = at_row // 8 % 2 == at_lane // 64
    fold = jnp.where(
        lax.broadcasted_iota(I32, (ENTRIES, rows), 1) // 16
        == lax.broadcasted_iota(I32, (ENTRIES, rows), 0),
        1.0,
        0.0,
    ).astype(BF16)
    unfold = jnp.where(
        lax.broadcasted_iota(I32, (rows, ENTRIES), 0) // 16
        == lax.broadcasted_iota(I32, (rows, ENTRIES), 1),
        1.0,
        0.0,
    ).astype(BF16)
    cell = lax.broadcasted_iota(I32, (ENTRIES, 128), 1) % 8

    def pieces(sections, place_yz):
        drop = upright(place_yz[0:1, :]).astype(F32)
        turn = upright(place_yz[1:2, :])
        drop_rows = jnp.dot(
            unfold, jnp.broadcast_to(drop, (ENTRIES, 128)).astype(BF16), preferred_element_type=F32
        ).astype(I32)
        keep = jnp.logical_and(((at_row - drop_rows) & 7) == at_lane // 8 % 8, right_plane)
        made = []
        for section in sections:
            wide = jnp.dot(windows[section].astype(BF16), spread, preferred_element_type=F32)
            wide = jnp.where(keep, wide, 0.0).astype(BF16)
            piece = jnp.dot(fold, wide, preferred_element_type=F32)
            for s in (1, 2, 4):
                moved = jnp.where(
                    cell + s < 8, pltpu.roll(piece, 128 - s, 1), pltpu.roll(piece, 8 - s, 1)
                )
                piece = jnp.where((turn & s) > 0, moved, piece)
            made.append(piece)
        return made

    own_piece = pieces((0, 1), own_off[5:7, 0:ENTRIES])
    for copy in off_copies:
        copy.wait()
    other_scalars = [
        pltpu.make_async_copy(other_off.at[n], off_s.at[n + 1], copy_sem.at[n + 2]) for n in range(2)
    ]
    for copy in other_scalars:
        copy.start()
    table_scalars.wait()

    def write_id(d, carry):
        ids[d] = jnp.full((1, 128), table_s[1, d], I32)
        return carry

    lax.fori_loop(0, DEVICES, write_id, 0)
    for copy in other_scalars:
        copy.wait()
    lax.fori_loop(0, ENTRIES // 4, cut_others, 0)
    to_right[...] = pieces((2,), other_off[0, 5:7, 0:ENTRIES])[0].astype(BF16)
    to_left[...] = pieces((3,), other_off[1, 5:7, 0:ENTRIES])[0].astype(BF16)
    near = (
        pltpu.make_async_remote_copy(to_right, low, near_send.at[0], near_recv.at[0], above, MESH),
        pltpu.make_async_remote_copy(to_left, high, near_send.at[1], near_recv.at[1], below, MESH),
    )
    for copy in near:
        copy.start()

    def id_copy(target):
        return pltpu.make_async_remote_copy(
            ids.at[target], received_ids.at[me], id_send, id_recv, place_of(target), MESH
        )

    def block_copy(target):
        return pltpu.make_async_remote_copy(
            blocks.at[target], received.at[me], send, recv, place_of(target), MESH
        )

    def send_id(k, carry):
        id_copy((me + k) % DEVICES).start()
        return carry

    lax.fori_loop(1, DEVICES, send_id, 0)
    own_id = pltpu.make_async_copy(ids.at[me], received_ids.at[me], local.at[0])
    own_id.start()
    for copy in near:
        copy.wait()
    whole = jnp.concatenate(
        [low[...].astype(F32), own_piece[0], own_piece[1], high[...].astype(F32)], axis=1
    )
    cubes[...] = jnp.where(
        at_x == 0, whole[:, 0:384], jnp.where(at_x == 1, whole[:, 64:448], whole[:, 128:512])
    )
    for copy in loads[1:]:
        copy.wait()

    def make(target):
        e = table_s[0, target]
        weighted = left_v[e] * cubes[pl.ds(e, 1), :].astype(BF16)
        block = lax.dot_general(
            weighted, right_v[e], (((1,), (1,)), ((), ())), preferred_element_type=F32
        )
        blocks[target] = block.astype(BF16)

    def target_at(k):
        return (me + k * STRIDE) % DEVICES

    make(target_at(1))

    def step(k, carry):
        make(target_at(k))
        block_copy(target_at(k - 1)).start()
        return carry

    lax.fori_loop(2, SPLIT, step, 0)
    for copy in den_copies[1]:
        copy.start()
    lax.fori_loop(SPLIT, DEVICES, step, 0)
    make(me)
    block_copy(target_at(DEVICES - 1)).start()
    own_block = pltpu.make_async_copy(blocks.at[me], received.at[me], local.at[1])
    own_block.start()
    own_id.wait()
    keep_den.wait()
    own_block.wait()
    all_but_one = pl.ds(0, DEVICES - 1)
    ids_done = pltpu.make_async_remote_copy(
        ids.at[all_but_one], received_ids.at[all_but_one], id_send, id_recv, above, MESH
    )
    blocks_done = pltpu.make_async_remote_copy(
        blocks.at[all_but_one], received.at[all_but_one], send, recv, above, MESH
    )
    ids_done.wait()
    for half in range(2):
        for copy in den_copies[half]:
            copy.wait()
    blocks_done.wait()


def exchange(offsets, pairs, live, pattern, pot, density, left, right):
    dma = pltpu.SemaphoreType.DMA
    return pl.pallas_call(
        exchange_kernel,
        name="exchange",
        out_shape=(
            jax.ShapeDtypeStruct((DEVICES, NB, NB), BF16),
            jax.ShapeDtypeStruct((DEVICES, 1, 128), I32),
            jax.ShapeDtypeStruct((4, TILE_R, TILE_C), BF16),
        ),
        in_specs=[vmem(), vmem(), smem(), smem()] + [hbm()] * 4,
        out_specs=(hbm(), hbm(), hbm()),
        scratch_shapes=[
            pltpu.VMEM((4, 4, 64, 8, 128), F32),
            pltpu.VMEM((TILE_R, TILE_C), BF16),
            pltpu.VMEM((ENTRIES, NB, CELLS), BF16),
            pltpu.VMEM((ENTRIES, NB, CELLS), BF16),
            pltpu.VMEM((4, ENTRIES * 16, 128), F32),
            pltpu.VMEM((8, 128), I32),
            pltpu.VMEM((2, 8, 128), I32),
            pltpu.SMEM((3, 8, 128), I32),
            pltpu.VMEM((8, 128), I32),
            pltpu.SMEM((8, 128), I32),
            pltpu.VMEM((DEVICES, 1, 128), I32),
            pltpu.VMEM((ENTRIES, 128), BF16),
            pltpu.VMEM((ENTRIES, 128), BF16),
            pltpu.VMEM((ENTRIES, 128), BF16),
            pltpu.VMEM((ENTRIES, 128), BF16),
            pltpu.VMEM((ENTRIES, CELLS), F32),
            pltpu.VMEM((DEVICES, NB, NB), BF16),
            dma((7,)), dma((2,)), dma((2,)), dma((4,)), dma((2,)), dma((2,)),
            dma, dma, dma, dma, dma((4, 2)), dma((4, 2)), dma((3,)),
        ],
        compiler_params=pltpu.CompilerParams(
            has_side_effects=True, vmem_limit_bytes=48 << 20, collective_id=0
        ),
    )(offsets, pairs, live, pattern, pot, density, left, right)


def combine_kernel(pattern, corner, ids_hbm, received, core, ham, total, ids, sem):
    copy = pltpu.make_async_copy(ids_hbm, ids, sem)
    copy.start()
    total[...] = jnp.zeros(total.shape, F32)
    copy.wait()

    def add(s, carry):
        slot = ids[s, 0, 0]

        @pl.when(slot >= 0)
        def _():
            total[slot] += received[s].astype(F32)

        return carry

    lax.fori_loop(0, DEVICES, add, 0)
    for i in range(ATOM_ROWS):
        for j in range(ATOM_COLS):
            on = pattern[corner[0] + i, corner[1] + j] > 0
            box = (slice(i * NB, (i + 1) * NB), slice(j * NB, (j + 1) * NB))

            @pl.when(on)
            def _():
                ham[box] = (core[box].astype(F32) + total[i * ATOM_COLS + j]).astype(BF16)

            @pl.when(jnp.logical_not(on))
            def _():
                ham[box] = jnp.zeros((NB, NB), BF16)


def combine(pattern, corner, ids, received, core):
    return pl.pallas_call(
        combine_kernel,
        name="combine",
        out_shape=jax.ShapeDtypeStruct((TILE_R, TILE_C), BF16),
        in_specs=[smem(), smem(), hbm(), vmem(), vmem()],
        out_specs=vmem(),
        scratch_shapes=[
            pltpu.VMEM((LOCAL, NB, NB), F32),
            pltpu.SMEM((DEVICES, 1, 128), I32),
            pltpu.SemaphoreType.DMA,
        ],
        compiler_params=pltpu.CompilerParams(vmem_limit_bytes=48 << 20),
    )(pattern, corner, ids, received, core)


def product_kernel(ham, den, out, hbuf, dbuf, load, hsend, dsend, csend, hrecv, drecv):
    row = lax.axis_index("row")
    col = lax.axis_index("col")
    core = row % 2
    z = row // 2 % 4
    ylo = row // 8
    x = col // 2
    yhi = col % 2

    def col_of(x_, h_):
        return x_ % 4 * 2 + h_

    def row_of(l_, z_, c_):
        return l_ * 8 + z_ % 4 * 2 + c_

    def h_at(c, half):
        return hbuf.at[c, pl.ds(half * HALF, HALF), :]

    def d_at(r, half):
        start = pl.multiple_of(r % 2 * TILE_R + half * HALF, HALF)
        return dbuf.at[r // 2, pl.ds(start, HALF), :]

    sent = []

    def h_copy(c, half, target, sem):
        return pltpu.make_async_remote_copy(
            h_at(c, half), h_at(c, half), sem, hrecv.at[c, half], (row, target), MESH
        )

    def d_copy(r, half, target, sem):
        return pltpu.make_async_remote_copy(
            d_at(r, half), d_at(r, half), sem, drecv.at[r, half], (target, col), MESH
        )

    count = {"h": 0, "d": 0, "c": 0}

    def push(kind, make, block, half, target):
        sems = {"h": hsend, "d": dsend, "c": csend}[kind]
        copy = make(block, half, target, sems.at[count[kind]])
        count[kind] += 1
        copy.start()
        sent.append(copy)

    def h_wait(c, half):
        h_copy(c, half, col, hsend.at[0]).wait_recv()

    def d_wait(r, half):
        d_copy(r, half, row, dsend.at[0]).wait_recv()

    other_core = row_of(ylo, z, 1 - core)
    h_partner = col_of(x, 1 - yhi)
    d_partner = row_of(1 - ylo, z, core)
    x_up, x_down = col_of(x + 1, yhi), col_of(x + 3, yhi)
    z_up, z_down = row_of(ylo, z + 1, core), row_of(ylo, z + 3, core)
    h_up, h_down = col_of(x + 1, 1 - yhi), col_of(x + 3, 1 - yhi)
    d_up, d_down = row_of(1 - ylo, z + 1, core), row_of(1 - ylo, z + 3, core)

    first = [pltpu.make_async_copy(ham, hbuf.at[col], load.at[0])] + [
        pltpu.make_async_copy(
            den.at[n],
            dbuf.at[r // 2, pl.ds(pl.multiple_of(core * TILE_R, TILE_R), TILE_R), :],
            load.at[n + 1],
        )
        for n, r in enumerate((row, d_partner, z_down, z_up))
    ]
    for copy in first:
        copy.start()
    barrier = pltpu.get_barrier_semaphore()
    for peer in (
        (row, x_up), (row, x_down), (row, h_partner), (z_up, col), (z_down, col), (other_core, col)
    ):
        pl.semaphore_signal(barrier, inc=1, device_id=peer, device_id_type=MESH)
    for copy in first:
        copy.wait()
    pl.semaphore_wait(barrier, 6)

    def share(r, half):
        push("c", d_copy, r, half, other_core)

    def h_both(c):
        for n in range(2):
            h_wait(c, n)

    def d_both(r):
        for n in range(2):
            d_wait(r, n)

    def multiply(k, start, half=None):
        lines = slice(None) if half is None else slice(half * HALF, (half + 1) * HALF)

        def tile(n, carry):
            columns = pl.ds(pl.multiple_of(n * 256, 256), 256)
            part = jnp.dot(hbuf[k, lines], dbuf[k, :, columns], preferred_element_type=F32)
            if start:
                out[lines, columns] = part
            else:
                out[lines, columns] += part
            return carry

        lax.fori_loop(0, TILE_C // 256, tile, 0)

    for n in range(2):
        push("h", h_copy, col, n, x_up)
        push("h", h_copy, col, 1 - n, x_down)
        push("h", h_copy, col, n, h_partner)
    push("d", d_copy, d_partner, 0, z_up)
    push("d", d_copy, d_partner, 1, z_down)
    push("d", d_copy, z_down, 0, z_up)
    push("d", d_copy, z_up, 1, z_down)
    push("d", d_copy, d_partner, 1, z_up)
    push("d", d_copy, d_partner, 0, z_down)
    for r in (row, d_partner, z_down, z_up):
        for n in range(2):
            share(r, n)

    h_wait(x_down, 0)
    push("h", h_copy, x_down, 0, x_up)
    h_wait(x_up, 1)
    push("h", h_copy, x_up, 1, x_down)
    h_wait(h_partner, 0)
    push("h", h_copy, h_partner, 0, x_up)
    push("h", h_copy, h_partner, 0, x_down)
    d_wait(d_down, 0)
    push("d", d_copy, d_down, 0, z_up)
    d_wait(d_up, 1)
    push("d", d_copy, d_up, 1, z_down)
    share(d_down, 0)
    share(d_up, 1)
    h_wait(h_partner, 1)
    push("h", h_copy, h_partner, 1, x_up)
    push("h", h_copy, h_partner, 1, x_down)
    for n in range(2):
        far = row_of(ylo, z + 2, core)
        d_wait(far, n)
        share(far, n)
    d_wait(d_down, 1)
    share(d_down, 1)
    d_wait(d_up, 0)
    share(d_up, 0)
    h_wait(x_down, 1)
    h_wait(x_up, 0)
    for n in range(2):
        far = col_of(x + 2, yhi)
        h_wait(far, n)
        push("h", h_copy, far, n, h_partner)
    for n in range(4):
        d_both(row_of(ylo, z + n, 1 - core))
    multiply(ylo * 4 + yhi, True)
    multiply(ylo * 4 + 2 + yhi, False)
    for n in range(2):
        far = row_of(1 - ylo, z + 2, core)
        d_wait(far, n)
        share(far, n)
    for n in range(4):
        d_both(row_of(1 - ylo, z + n, 1 - core))
    multiply((1 - ylo) * 4 + yhi, False)
    multiply((1 - ylo) * 4 + 2 + yhi, False)
    multiply(h_partner, False)
    for half in range(2):
        for c in (h_down, h_up):
            h_wait(c, half)
            multiply(c, False, half)
    for half in range(2):
        far = col_of(x + 2, 1 - yhi)
        h_wait(far, half)
        multiply(far, False, half)
    for copy in sent:
        copy.wait_send()


def multiply_all(ham, den):
    return pl.pallas_call(
        product_kernel,
        name="product",
        out_shape=jax.ShapeDtypeStruct((TILE_R, TILE_C), F32),
        in_specs=[hbm(), hbm()],
        out_specs=vmem(),
        scratch_shapes=[
            pltpu.VMEM((COLS, TILE_R, TILE_C), BF16),
            pltpu.VMEM((COLS, 2 * TILE_R, TILE_C), BF16),
            pltpu.SemaphoreType.DMA((5,)),
            pltpu.SemaphoreType.DMA((16,)),
            pltpu.SemaphoreType.DMA((16,)),
            pltpu.SemaphoreType.DMA((16,)),
            pltpu.SemaphoreType.DMA((COLS, 2)),
            pltpu.SemaphoreType.DMA((ROWS, 2)),
        ],
        compiler_params=pltpu.CompilerParams(
            has_side_effects=True, vmem_limit_bytes=56 << 20, collective_id=1
        ),
    )(ham, den)


def shards(
    potential, basis_left, basis_right, core_matrix, density, pattern, pair_atoms, cube_offsets, live_count
):
    corner = jnp.stack([lax.axis_index("row") * ATOM_ROWS, lax.axis_index("col") * ATOM_COLS]).astype(I32)
    received, received_ids, near_den = exchange(
        cube_offsets.T, pair_atoms.T, live_count, pattern, potential.reshape(4, 64, 8, 512), density, basis_left, basis_right
    )
    ham = combine(pattern, corner, received_ids, received, core_matrix)
    return ham, multiply_all(ham, near_den)


def solution(mesh):
    flat = ("row", "col")
    tile = P("row", "col")
    placed = (
        P(flat, None, None),
        P(flat, None, None),
        P(flat, None, None),
        tile,
        tile,
        P(),
        P(flat, None),
        P(flat, None),
        P(flat),
    )
    return jax.shard_map(
        shards, mesh=mesh, in_specs=placed, out_specs=(tile, tile), check_vma=False
    )
```

```python
import functools

import jax
import jax.numpy as jnp
from jax import lax
from jax.experimental import pallas as pl
from jax.experimental.pallas import tpu as pltpu
from jax.sharding import PartitionSpec as P

NATOMS = 64
NB = 128
CELLS = 384
ROWS = 16
COLS = 8
DEVICES = 128
ENTRIES = 64
ATOM_ROWS = 4
ATOM_COLS = 8
LOCAL = ATOM_ROWS * ATOM_COLS
TILE_R = 512
TILE_C = 1024
HALF = 256
STRIDE = 51
MESH = pl.DeviceIdType.MESH
F32 = jnp.float32
BF16 = jnp.bfloat16
I32 = jnp.int32


def vmem():
    return pl.BlockSpec(memory_space=pltpu.VMEM)


def smem():
    return pl.BlockSpec(memory_space=pltpu.SMEM)


def hbm():
    return pl.BlockSpec(memory_space=pl.ANY)


def far_hbm():
    return pl.BlockSpec(memory_space=pltpu.HBM)


def place_of(index):
    return (index // COLS, index % COLS)


def exchange_kernel(
    offsets_h, pairs_h, live, pattern_h, pot, density, left, right,
    received, info, near_den,
    offsets, pairs, pattern, received_ids, pot_v, den_v, left_v, right_v, windows, own_off, other_off, off_s, table, table_s, ids,
    to_right, to_left, low, high, cubes, blocks,
    load_sem, off_send, off_recv, copy_sem, near_send, near_recv, send, recv, id_send, id_recv,
    den_send, den_recv, local, small_sem, entered,
):
    row = lax.axis_index("row")
    col = lax.axis_index("col")
    me = row * COLS + col
    above = place_of((me + 1) % DEVICES)
    below = place_of((me + DEVICES - 1) % DEVICES)

    loads = [
        pltpu.make_async_copy(a, b, load_sem.at[n])
        for n, (a, b) in enumerate(((density, den_v), (left, left_v), (right, right_v)))
    ]
    pot_loads = [
        pltpu.make_async_copy(
            pot.at[:, :, :, pl.ds(n * 128, 128)], pot_v.at[n], load_sem.at[n + 3]
        )
        for n in range(4)
    ]
    small = [
        pltpu.make_async_copy(a, b, small_sem.at[n])
        for n, (a, b) in enumerate(((offsets_h, offsets), (pairs_h, pairs), (pattern_h, pattern)))
    ]
    for copy in small + loads[:1] + pot_loads + loads[1:]:
        copy.start()
    barrier = pltpu.get_barrier_semaphore()

    def greet(device):
        pl.semaphore_signal(barrier, inc=1, device_id=device, device_id_type=MESH)

    def greet_row(k, carry):
        greet((row, (col + k) % COLS))
        return carry

    def greet_col(k, carry):
        greet(((row + k) % ROWS, col))
        return carry

    greet(above)
    greet(below)
    lax.fori_loop(1, COLS, greet_row, 0)
    lax.fori_loop(1, ROWS, greet_col, 0)

    for copy in small:
        copy.wait()
    own_off[...] = jnp.zeros((8, 128), I32)
    own_off[0:1, 0:ENTRIES] = offsets[0:1, :]
    own_y = offsets[1:2, :]
    own_z = offsets[2:3, :]
    for n, value in enumerate(
        (
            own_y >> 3,
            jnp.minimum((own_y >> 3) + 1, 63),
            own_z >> 7,
            jnp.minimum((own_z >> 7) + 1, 3),
            own_y & 7,
            own_z & 127,
        )
    ):
        own_off[n + 1 : n + 2, 0:ENTRIES] = value
    own_scalars = pltpu.make_async_copy(own_off, off_s.at[0], copy_sem.at[0])
    own_scalars.start()

    entry = lax.broadcasted_iota(I32, (ENTRIES, ENTRIES), 0)
    eye = entry == lax.broadcasted_iota(I32, (ENTRIES, ENTRIES), 1)

    def upright(line):
        return jnp.sum(jnp.where(eye, line, 0), axis=1, keepdims=True)

    first = pairs[0:1, :]
    second = pairs[1:2, :]
    owner = upright(first // ATOM_ROWS * COLS + second // ATOM_COLS)
    place = upright(first % ATOM_ROWS * ATOM_COLS + second % ATOM_COLS)
    at_x = upright(offsets[0:1, :])
    ordinal = lax.broadcasted_iota(I32, (ENTRIES, DEVICES), 0)
    target_of = lax.broadcasted_iota(I32, (ENTRIES, DEVICES), 1)
    named = jnp.logical_and(owner == target_of, ordinal < live[0])
    table[...] = jnp.zeros((8, 128), I32)
    table[0:1, :] = jnp.sum(jnp.where(named, ordinal, 0), axis=0, keepdims=True)
    table[1:2, :] = jnp.sum(jnp.where(named, place + 1, 0), axis=0, keepdims=True) - 1
    table_scalars = pltpu.make_async_copy(table, table_s, copy_sem.at[1])
    table_scalars.start()

    loads[0].wait()
    pick_rows = (
        lax.broadcasted_iota(I32, (8, NATOMS), 1)
        == row * ATOM_ROWS + lax.broadcasted_iota(I32, (8, NATOMS), 0)
    )
    pick_cols = (
        lax.broadcasted_iota(I32, (NATOMS, TILE_C), 0)
        == col * ATOM_COLS + lax.broadcasted_iota(I32, (NATOMS, TILE_C), 1) // NB
    )
    pick_again = (
        lax.broadcasted_iota(I32, (NATOMS, 128), 0)
        == col * ATOM_COLS + lax.broadcasted_iota(I32, (NATOMS, 128), 1) % ATOM_COLS
    )

    def flags(chosen):
        return jnp.where(chosen, 1.0, 0.0).astype(BF16)

    on_rows = jnp.dot(flags(pick_rows), flags(pattern[...] > 0), preferred_element_type=F32).astype(BF16)
    on_wide = jnp.dot(on_rows, flags(pick_cols), preferred_element_type=F32)
    on_again = jnp.dot(on_rows, flags(pick_again), preferred_element_type=F32)
    mine = (
        lax.broadcasted_iota(I32, (8, 128), 1) // ATOM_COLS == lax.broadcasted_iota(I32, (8, 128), 0)
    )
    info[...] = jnp.zeros((8, 128), I32)
    info[1:2, :] = jnp.sum(
        jnp.where(jnp.logical_and(mine, on_again > 0.0), 1, 0), axis=0, keepdims=True
    )
    for i in range(ATOM_ROWS):
        lines = slice(i * NB, (i + 1) * NB)
        den_v[lines] = jnp.where(on_wide[i : i + 1, :] > 0.0, den_v[lines].astype(F32), 0.0).astype(BF16)
    keep_den = pltpu.make_async_copy(den_v, near_den.at[0], local.at[2])
    keep_den.start()

    lane = lax.broadcasted_iota(I32, (8, 128), 1)
    line = lax.broadcasted_iota(I32, (8, 128), 0)

    def cut(source, e, planes):
        y_tiles = (off_s[source, 1, e], off_s[source, 2, e])
        z_tiles = (off_s[source, 3, e], off_s[source, 4, e])
        drop = off_s[source, 5, e]
        turn = off_s[source, 6, e]
        kept = ((lane - turn) & 127) < 8
        for section, plane in planes:
            for p in range(2):
                quarter = [
                    [pot_v[zt, plane + p, yt] for zt in z_tiles] for yt in y_tiles
                ]
                upper, lower = [jnp.where(lane >= turn, a, b) for a, b in quarter]
                window = jnp.where(jnp.logical_and(line >= drop, kept), upper, 0.0)
                window = jnp.where(jnp.logical_and(line < drop, kept), lower, window)
                start = pl.multiple_of(e * 16 + p * 8, 8)
                windows[section, pl.ds(start, 8), :] = window

    def cut_own(e, carry):
        for n in range(4):
            cut(0, e * 4 + n, ((0, 0), (1, 2)))
        return carry

    def cut_others(e, carry):
        for n in range(4):
            cut(1, e * 4 + n, ((2, 2),))
            cut(2, e * 4 + n, ((3, 0),))
        return carry

    pl.semaphore_wait(barrier, ROWS + COLS)
    off_copies = (
        pltpu.make_async_remote_copy(
            own_off, other_off.at[0], off_send.at[0], off_recv.at[0], below, MESH
        ),
        pltpu.make_async_remote_copy(
            own_off, other_off.at[1], off_send.at[1], off_recv.at[1], above, MESH
        ),
    )
    for copy in off_copies:
        copy.start()

    def tell(k, carry):
        pl.semaphore_signal(
            entered, inc=1, device_id=(row, (col + k) % COLS), device_id_type=MESH
        )
        return carry

    lax.fori_loop(1, COLS, tell, 0)

    def den_copy(slot, half, device):
        part = pl.ds(half * HALF, HALF)
        return pltpu.make_async_remote_copy(
            den_v.at[part, :], near_den.at[slot, part, :],
            den_send.at[slot, half], den_recv.at[slot, half], device, MESH,
        )

    z = row // 2 % 4
    base = row - z * 2
    d_partner = ((row + 8) % ROWS, col)
    den_copies = (
        den_copy(1, 0, d_partner),
        den_copy(2, 0, (base + (z + 1) % 4 * 2, col)),
        den_copy(3, 1, (base + (z + 3) % 4 * 2, col)),
        den_copy(1, 1, d_partner),
    )
    for copy in den_copies[:3]:
        copy.start()

    own_scalars.wait()
    for copy in pot_loads:
        copy.wait()
    lax.fori_loop(0, ENTRIES // 4, cut_own, 0)

    at = lax.broadcasted_iota(I32, (128, 128), 0)
    to = lax.broadcasted_iota(I32, (128, 128), 1)
    spread = jnp.where(at % 8 == to % 8, 1.0, 0.0).astype(BF16)
    rows = ENTRIES * 16
    at_row = lax.broadcasted_iota(I32, (rows, 128), 0)
    at_lane = lax.broadcasted_iota(I32, (rows, 128), 1)
    right_plane = at_row // 8 % 2 == at_lane // 64
    fold = jnp.where(
        lax.broadcasted_iota(I32, (ENTRIES, rows), 1) // 16
        == lax.broadcasted_iota(I32, (ENTRIES, rows), 0),
        1.0,
        0.0,
    ).astype(BF16)
    unfold = jnp.where(
        lax.broadcasted_iota(I32, (rows, ENTRIES), 0) // 16
        == lax.broadcasted_iota(I32, (rows, ENTRIES), 1),
        1.0,
        0.0,
    ).astype(BF16)
    cell = lax.broadcasted_iota(I32, (ENTRIES, 128), 1) % 8

    def pieces(sections, place_yz):
        drop = upright(place_yz[0:1, :]).astype(F32)
        turn = upright(place_yz[1:2, :])
        drop_rows = jnp.dot(
            unfold, jnp.broadcast_to(drop, (ENTRIES, 128)).astype(BF16), preferred_element_type=F32
        ).astype(I32)
        keep = jnp.logical_and(((at_row - drop_rows) & 7) == at_lane // 8 % 8, right_plane)
        made = []
        for section in sections:
            wide = jnp.dot(windows[section].astype(BF16), spread, preferred_element_type=F32)
            wide = jnp.where(keep, wide, 0.0).astype(BF16)
            piece = jnp.dot(fold, wide, preferred_element_type=F32)
            for s in (1, 2, 4):
                moved = jnp.where(
                    cell + s < 8, pltpu.roll(piece, 128 - s, 1), pltpu.roll(piece, 8 - s, 1)
                )
                piece = jnp.where((turn & s) > 0, moved, piece)
            made.append(piece)
        return made

    own_piece = pieces((0, 1), own_off[5:7, 0:ENTRIES])
    for copy in off_copies:
        copy.wait()
    other_scalars = [
        pltpu.make_async_copy(other_off.at[n], off_s.at[n + 1], copy_sem.at[n + 2]) for n in range(2)
    ]
    for copy in other_scalars:
        copy.start()
    table_scalars.wait()

    own_lane = lax.broadcasted_iota(I32, (1, 128), 1) == me

    def write_id(d, carry):
        ids[d] = jnp.where(own_lane, jnp.full((1, 128), table_s[1, d] + 1, I32), 0)
        return carry

    lax.fori_loop(0, DEVICES, write_id, 0)
    for copy in other_scalars:
        copy.wait()
    lax.fori_loop(0, ENTRIES // 4, cut_others, 0)
    to_right[...] = pieces((2,), other_off[0, 5:7, 0:ENTRIES])[0].astype(BF16)
    to_left[...] = pieces((3,), other_off[1, 5:7, 0:ENTRIES])[0].astype(BF16)
    near = (
        pltpu.make_async_remote_copy(to_right, low, near_send.at[0], near_recv.at[0], above, MESH),
        pltpu.make_async_remote_copy(to_left, high, near_send.at[1], near_recv.at[1], below, MESH),
    )
    for copy in near:
        copy.start()

    def id_copy(target):
        return pltpu.make_async_remote_copy(
            ids.at[target], received_ids.at[me], id_send, id_recv, place_of(target), MESH
        )

    def block_copy(target):
        return pltpu.make_async_remote_copy(
            blocks.at[target], received.at[me], send, recv, place_of(target), MESH
        )

    def send_id(k, carry):
        id_copy((me + k) % DEVICES).start()
        return carry

    pl.semaphore_wait(entered, COLS - 1)
    den_copies[3].start()
    lax.fori_loop(1, DEVICES, send_id, 0)
    own_id = pltpu.make_async_copy(ids.at[me], received_ids.at[me], local.at[0])
    own_id.start()
    for copy in near:
        copy.wait()
    whole = jnp.concatenate(
        [low[...].astype(F32), own_piece[0], own_piece[1], high[...].astype(F32)], axis=1
    )
    cubes[...] = jnp.where(
        at_x == 0, whole[:, 0:384], jnp.where(at_x == 1, whole[:, 64:448], whole[:, 128:512])
    )
    for copy in loads[1:]:
        copy.wait()

    def make(target):
        e = table_s[0, target]
        weighted = left_v[e] * cubes[pl.ds(e, 1), :].astype(BF16)
        block = lax.dot_general(
            weighted, right_v[e], (((1,), (1,)), ((), ())), preferred_element_type=F32
        )
        blocks[target] = block.astype(BF16)

    def target_at(k):
        return (me + k * STRIDE) % DEVICES

    make(target_at(1))

    def step(k, carry):
        make(target_at(k))
        block_copy(target_at(k - 1)).start()
        return carry

    lax.fori_loop(2, DEVICES, step, 0)
    make(me)
    block_copy(target_at(DEVICES - 1)).start()
    own_block = pltpu.make_async_copy(blocks.at[me], received.at[me], local.at[1])
    own_block.start()
    own_id.wait()
    keep_den.wait()
    own_block.wait()
    all_but_one = pl.ds(0, DEVICES - 1)
    ids_done = pltpu.make_async_remote_copy(
        ids.at[all_but_one], received_ids.at[all_but_one], id_send, id_recv, above, MESH
    )
    blocks_done = pltpu.make_async_remote_copy(
        blocks.at[all_but_one], received.at[all_but_one], send, recv, above, MESH
    )
    ids_done.wait()
    info[0:1, :] = jnp.sum(received_ids[...], axis=0) - 1
    for copy in den_copies:
        copy.wait()
    blocks_done.wait()


def exchange(offsets, pairs, live, pattern, pot, density, left, right):
    dma = pltpu.SemaphoreType.DMA
    return pl.pallas_call(
        exchange_kernel,
        name="exchange",
        out_shape=(
            jax.ShapeDtypeStruct((DEVICES, NB, NB), BF16),
            jax.ShapeDtypeStruct((8, 128), I32),
            jax.ShapeDtypeStruct((4, TILE_R, TILE_C), BF16),
        ),
        in_specs=[far_hbm(), far_hbm(), smem()] + [far_hbm()] * 5,
        out_specs=(hbm(), vmem(), hbm()),
        scratch_shapes=[
            pltpu.VMEM((3, ENTRIES), I32),
            pltpu.VMEM((2, ENTRIES), I32),
            pltpu.VMEM((NATOMS, NATOMS), I32),
            pltpu.VMEM((DEVICES, 1, 128), I32),
            pltpu.VMEM((4, 4, 64, 8, 128), F32),
            pltpu.VMEM((TILE_R, TILE_C), BF16),
            pltpu.VMEM((ENTRIES, NB, CELLS), BF16),
            pltpu.VMEM((ENTRIES, NB, CELLS), BF16),
            pltpu.VMEM((4, ENTRIES * 16, 128), F32),
            pltpu.VMEM((8, 128), I32),
            pltpu.VMEM((2, 8, 128), I32),
            pltpu.SMEM((3, 8, 128), I32),
            pltpu.VMEM((8, 128), I32),
            pltpu.SMEM((8, 128), I32),
            pltpu.VMEM((DEVICES, 1, 128), I32),
            pltpu.VMEM((ENTRIES, 128), BF16),
            pltpu.VMEM((ENTRIES, 128), BF16),
            pltpu.VMEM((ENTRIES, 128), BF16),
            pltpu.VMEM((ENTRIES, 128), BF16),
            pltpu.VMEM((ENTRIES, CELLS), F32),
            pltpu.VMEM((DEVICES, NB, NB), BF16),
            dma((7,)), dma((2,)), dma((2,)), dma((4,)), dma((2,)), dma((2,)),
            dma, dma, dma, dma, dma((4, 2)), dma((4, 2)), dma((3,)),
            dma((3,)), pltpu.SemaphoreType.REGULAR,
        ],
        compiler_params=pltpu.CompilerParams(
            has_side_effects=True, vmem_limit_bytes=48 << 20, collective_id=0
        ),
    )(offsets, pairs, live, pattern, pot, density, left, right)


def combine_kernel(info, received, core, ham, head, after):
    def clear(b, carry):
        head[b] = -1
        return carry

    lax.fori_loop(0, LOCAL, clear, 0)

    def link(s, carry):
        slot = info[0, s]

        @pl.when(slot >= 0)
        def _():
            after[s] = head[slot]
            head[slot] = s

        return carry

    lax.fori_loop(0, DEVICES, link, 0)

    def more(state):
        s, total = state
        return after[s], total + received[s].astype(F32)

    for i in range(ATOM_ROWS):
        for j in range(ATOM_COLS):
            block = i * ATOM_COLS + j
            box = (slice(i * NB, (i + 1) * NB), slice(j * NB, (j + 1) * NB))
            on = info[1, block] > 0

            @pl.when(on)
            def _():
                total = lax.while_loop(
                    lambda state: state[0] >= 0, more, (head[block], core[box].astype(F32))
                )[1]
                ham[box] = total.astype(BF16)

            @pl.when(jnp.logical_not(on))
            def _():
                ham[box] = jnp.zeros((NB, NB), BF16)


def combine(info, received, core):
    return pl.pallas_call(
        combine_kernel,
        name="combine",
        out_shape=jax.ShapeDtypeStruct((TILE_R, TILE_C), BF16),
        in_specs=[smem(), vmem(), vmem()],
        out_specs=vmem(),
        scratch_shapes=[pltpu.SMEM((LOCAL,), I32), pltpu.SMEM((DEVICES,), I32)],
        compiler_params=pltpu.CompilerParams(vmem_limit_bytes=48 << 20),
    )(info, received, core)


def product_kernel(ham, den, out, hbuf, dbuf, load, hsend, dsend, csend, hrecv, drecv):
    row = lax.axis_index("row")
    col = lax.axis_index("col")
    core = row % 2
    z = row // 2 % 4
    ylo = row // 8
    x = col // 2
    yhi = col % 2

    def col_of(x_, h_):
        return x_ % 4 * 2 + h_

    def row_of(l_, z_, c_):
        return l_ * 8 + z_ % 4 * 2 + c_

    def h_at(c, half):
        return hbuf.at[c, pl.ds(half * HALF, HALF), :]

    def d_at(r, half):
        start = pl.multiple_of(r % 2 * TILE_R + half * HALF, HALF)
        return dbuf.at[r // 2, pl.ds(start, HALF), :]

    sent = []

    def h_copy(c, half, target, sem):
        return pltpu.make_async_remote_copy(
            h_at(c, half), h_at(c, half), sem, hrecv.at[c, half], (row, target), MESH
        )

    def d_copy(r, half, target, sem):
        return pltpu.make_async_remote_copy(
            d_at(r, half), d_at(r, half), sem, drecv.at[r, half], (target, col), MESH
        )

    count = {"h": 0, "d": 0, "c": 0}

    def push(kind, make, block, half, target):
        sems = {"h": hsend, "d": dsend, "c": csend}[kind]
        copy = make(block, half, target, sems.at[count[kind]])
        count[kind] += 1
        copy.start()
        sent.append(copy)

    def h_wait(c, half):
        h_copy(c, half, col, hsend.at[0]).wait_recv()

    def d_wait(r, half):
        d_copy(r, half, row, dsend.at[0]).wait_recv()

    other_core = row_of(ylo, z, 1 - core)
    h_partner = col_of(x, 1 - yhi)
    d_partner = row_of(1 - ylo, z, core)
    x_up, x_down = col_of(x + 1, yhi), col_of(x + 3, yhi)
    z_up, z_down = row_of(ylo, z + 1, core), row_of(ylo, z + 3, core)
    h_up, h_down = col_of(x + 1, 1 - yhi), col_of(x + 3, 1 - yhi)
    d_up, d_down = row_of(1 - ylo, z + 1, core), row_of(1 - ylo, z + 3, core)

    first = [pltpu.make_async_copy(ham, hbuf.at[col], load.at[0])] + [
        pltpu.make_async_copy(
            den.at[slot, pl.ds(half * HALF, HALF), :], d_at(r, half), load.at[n + 1]
        )
        for n, (slot, r, half) in enumerate(
            ((0, row, 0), (0, row, 1), (1, d_partner, 0), (1, d_partner, 1), (2, z_down, 0), (3, z_up, 1))
        )
    ]
    for copy in first:
        copy.start()
    barrier = pltpu.get_barrier_semaphore()
    for peer in (
        (row, x_up), (row, x_down), (row, h_partner), (z_up, col), (z_down, col), (other_core, col)
    ):
        pl.semaphore_signal(barrier, inc=1, device_id=peer, device_id_type=MESH)
    for copy in first:
        copy.wait()
    pl.semaphore_wait(barrier, 6)

    def share(r, half):
        push("c", d_copy, r, half, other_core)

    def h_both(c):
        for n in range(2):
            h_wait(c, n)

    def d_both(r):
        for n in range(2):
            d_wait(r, n)

    def multiply(k, start, half=None):
        if half is None:
            lines = slice(None)
        else:
            lines = pl.ds(pl.multiple_of(half * HALF, HALF), HALF)

        def tile(n, carry):
            columns = pl.ds(pl.multiple_of(n * 256, 256), 256)
            part = jnp.dot(hbuf[k, lines], dbuf[k, :, columns], preferred_element_type=F32)
            if start:
                out[lines, columns] = part
            else:
                out[lines, columns] += part
            return carry

        lax.fori_loop(0, TILE_C // 256, tile, 0)

    for n in range(2):
        push("h", h_copy, col, n, x_up)
        push("h", h_copy, col, 1 - n, x_down)
        push("h", h_copy, col, n, h_partner)
    push("d", d_copy, row, 1, z_up)
    push("d", d_copy, row, 0, z_down)
    push("d", d_copy, d_partner, 0, z_up)
    push("d", d_copy, d_partner, 1, z_down)
    push("d", d_copy, z_down, 0, z_up)
    push("d", d_copy, z_up, 1, z_down)
    push("d", d_copy, d_partner, 1, z_up)
    push("d", d_copy, d_partner, 0, z_down)
    for r, half in ((row, 0), (row, 1), (d_partner, 0), (d_partner, 1), (z_down, 0), (z_up, 1)):
        share(r, half)

    h_wait(x_down, 0)
    push("h", h_copy, x_down, 0, x_up)
    h_wait(x_up, 1)
    push("h", h_copy, x_up, 1, x_down)
    h_wait(h_partner, 0)
    push("h", h_copy, h_partner, 0, x_up)
    push("h", h_copy, h_partner, 0, x_down)
    d_wait(z_down, 1)
    share(z_down, 1)
    d_wait(z_up, 0)
    share(z_up, 0)
    d_wait(d_down, 0)
    push("d", d_copy, d_down, 0, z_up)
    d_wait(d_up, 1)
    push("d", d_copy, d_up, 1, z_down)
    share(d_down, 0)
    share(d_up, 1)
    h_wait(h_partner, 1)
    push("h", h_copy, h_partner, 1, x_up)
    push("h", h_copy, h_partner, 1, x_down)
    h_wait(x_down, 1)
    h_wait(x_up, 0)
    for n in range(2):
        far = row_of(ylo, z + 2, core)
        d_wait(far, n)
        share(far, n)
    for n in range(2):
        far = col_of(x + 2, yhi)
        h_wait(far, n)
        push("h", h_copy, far, n, h_partner)
    for n in range(4):
        d_both(row_of(ylo, z + n, 1 - core))
    multiply(ylo * 4 + yhi, True)
    multiply(ylo * 4 + 2 + yhi, False)
    d_wait(d_down, 1)
    share(d_down, 1)
    d_wait(d_up, 0)
    share(d_up, 0)
    for n in (0, 1, 3):
        d_both(row_of(1 - ylo, z + n, 1 - core))

    h_far = col_of(x + 2, 1 - yhi)
    late = (1 - ylo) * 4 + (z + 2) % 4
    ready = (1 - ylo) * 4 + yhi
    units = [(k, half) for k in (ready, ready + 2, h_partner) for half in range(2)]
    units += [(k, half) for half in range(2) for k in (h_down, h_up)]
    units += [(h_far, half) for half in range(2)]
    passed = 0
    spots = []
    for k, half in units:
        is_late = jnp.where(k == late, 1, 0)
        spots.append((is_late, len(spots) - passed))
        passed = passed + is_late

    def d_late(n):
        far = row_of(1 - ylo, z + 2, core)
        d_wait(far, n)
        share(far, n)

    for spot in range(len(units) - 2):
        if 6 <= spot + 2:
            h_wait(*units[spot + 2])
        if spot in (6, 7):
            d_late(spot - 6)
        k = 0
        half = 0
        for (unit_k, unit_half), (is_late, at) in zip(units, spots):
            here = jnp.where(at == spot, 1 - is_late, 0)
            k = k + here * unit_k
            half = half + here * unit_half
        multiply(k, False, half)
    d_both(row_of(1 - ylo, z + 2, 1 - core))
    multiply(late, False)
    for copy in sent:
        copy.wait_send()


def multiply_all(ham, den):
    return pl.pallas_call(
        product_kernel,
        name="product",
        out_shape=jax.ShapeDtypeStruct((TILE_R, TILE_C), F32),
        in_specs=[hbm(), hbm()],
        out_specs=vmem(),
        scratch_shapes=[
            pltpu.VMEM((COLS, TILE_R, TILE_C), BF16),
            pltpu.VMEM((COLS, 2 * TILE_R, TILE_C), BF16),
            pltpu.SemaphoreType.DMA((7,)),
            pltpu.SemaphoreType.DMA((16,)),
            pltpu.SemaphoreType.DMA((16,)),
            pltpu.SemaphoreType.DMA((16,)),
            pltpu.SemaphoreType.DMA((COLS, 2)),
            pltpu.SemaphoreType.DMA((ROWS, 2)),
        ],
        compiler_params=pltpu.CompilerParams(
            has_side_effects=True, vmem_limit_bytes=40 << 20, collective_id=1
        ),
    )(ham, den)


def shards(
    potential, basis_left, basis_right, core_matrix, density, pattern, pair_atoms, cube_offsets, live_count
):
    received, info, near_den = exchange(
        cube_offsets.T, pair_atoms.T, live_count, pattern, potential.reshape(4, 64, 8, 512),
        density, basis_left, basis_right,
    )
    ham = combine(info, received, core_matrix)
    return ham, multiply_all(ham, near_den)


def solution(mesh):
    flat = ("row", "col")
    tile = P("row", "col")
    placed = (
        P(flat, None, None),
        P(flat, None, None),
        P(flat, None, None),
        tile,
        tile,
        P(),
        P(flat, None),
        P(flat, None),
        P(flat),
    )
    return jax.shard_map(
        shards, mesh=mesh, in_specs=placed, out_specs=(tile, tile), check_vma=False
    )
```

```python
import functools

import jax
import jax.numpy as jnp
from jax import lax
from jax.experimental import pallas as pl
from jax.experimental.pallas import tpu as pltpu
from jax.sharding import PartitionSpec as P

NATOMS = 64
NB = 128
CELLS = 384
ROWS = 16
COLS = 8
DEVICES = 128
ENTRIES = 64
ATOM_ROWS = 4
ATOM_COLS = 8
LOCAL = ATOM_ROWS * ATOM_COLS
TILE_R = 512
TILE_C = 1024
HALF = 256
STRIDE = 51
MESH = pl.DeviceIdType.MESH
F32 = jnp.float32
BF16 = jnp.bfloat16
I32 = jnp.int32


def vmem():
    return pl.BlockSpec(memory_space=pltpu.VMEM)


def smem():
    return pl.BlockSpec(memory_space=pltpu.SMEM)


def hbm():
    return pl.BlockSpec(memory_space=pl.ANY)


def far_hbm():
    return pl.BlockSpec(memory_space=pltpu.HBM)


def place_of(index):
    return (index // COLS, index % COLS)


def exchange_kernel(
    offsets_h, pairs_h, live, pattern_h, pot, density, left, right,
    received, info, near_den,
    offsets, pairs, pattern, received_ids, pot_v, den_v, left_v, right_v, windows, own_off, other_off, off_s, table, table_s, ids,
    to_right, to_left, low, high, cubes, blocks,
    load_sem, off_send, off_recv, copy_sem, near_send, near_recv, send, recv, id_send, id_recv,
    den_send, den_recv, local, small_sem, entered,
):
    row = lax.axis_index("row")
    col = lax.axis_index("col")
    me = row * COLS + col
    above = place_of((me + 1) % DEVICES)
    below = place_of((me + DEVICES - 1) % DEVICES)

    loads = [
        pltpu.make_async_copy(a, b, load_sem.at[n])
        for n, (a, b) in enumerate(((density, den_v), (left, left_v), (right, right_v)))
    ]
    pot_loads = [
        pltpu.make_async_copy(
            pot.at[:, :, :, pl.ds(n * 128, 128)], pot_v.at[n], load_sem.at[n + 3]
        )
        for n in range(4)
    ]
    small = [
        pltpu.make_async_copy(a, b, small_sem.at[n])
        for n, (a, b) in enumerate(((offsets_h, offsets), (pairs_h, pairs), (pattern_h, pattern)))
    ]
    for copy in small + loads[:1] + pot_loads + loads[1:]:
        copy.start()
    barrier = pltpu.get_barrier_semaphore()

    def greet(device):
        pl.semaphore_signal(barrier, inc=1, device_id=device, device_id_type=MESH)

    def greet_row(k, carry):
        greet((row, (col + k) % COLS))
        return carry

    def greet_col(k, carry):
        greet(((row + k) % ROWS, col))
        return carry

    greet(above)
    greet(below)
    lax.fori_loop(1, COLS, greet_row, 0)
    lax.fori_loop(1, ROWS, greet_col, 0)

    for copy in small:
        copy.wait()
    own_off[...] = jnp.zeros((8, 128), I32)
    own_off[0:1, 0:ENTRIES] = offsets[0:1, :]
    own_y = offsets[1:2, :]
    own_z = offsets[2:3, :]
    for n, value in enumerate(
        (
            own_y >> 3,
            jnp.minimum((own_y >> 3) + 1, 63),
            own_z >> 7,
            jnp.minimum((own_z >> 7) + 1, 3),
            own_y & 7,
            own_z & 127,
        )
    ):
        own_off[n + 1 : n + 2, 0:ENTRIES] = value
    own_scalars = pltpu.make_async_copy(own_off, off_s.at[0], copy_sem.at[0])
    own_scalars.start()

    entry = lax.broadcasted_iota(I32, (ENTRIES, ENTRIES), 0)
    eye = entry == lax.broadcasted_iota(I32, (ENTRIES, ENTRIES), 1)

    def upright(line):
        return jnp.sum(jnp.where(eye, line, 0), axis=1, keepdims=True)

    first = pairs[0:1, :]
    second = pairs[1:2, :]
    owner = upright(first // ATOM_ROWS * COLS + second // ATOM_COLS)
    place = upright(first % ATOM_ROWS * ATOM_COLS + second % ATOM_COLS)
    at_x = upright(offsets[0:1, :])
    ordinal = lax.broadcasted_iota(I32, (ENTRIES, DEVICES), 0)
    target_of = lax.broadcasted_iota(I32, (ENTRIES, DEVICES), 1)
    named = jnp.logical_and(owner == target_of, ordinal < live[0])
    table[...] = jnp.zeros((8, 128), I32)
    table[0:1, :] = jnp.sum(jnp.where(named, ordinal, 0), axis=0, keepdims=True)
    table[1:2, :] = jnp.sum(jnp.where(named, place + 1, 0), axis=0, keepdims=True) - 1
    table_scalars = pltpu.make_async_copy(table, table_s, copy_sem.at[1])
    table_scalars.start()

    lane = lax.broadcasted_iota(I32, (8, 128), 1)
    line = lax.broadcasted_iota(I32, (8, 128), 0)

    def cut(source, e, planes):
        y_tiles = (off_s[source, 1, e], off_s[source, 2, e])
        z_tiles = (off_s[source, 3, e], off_s[source, 4, e])
        drop = off_s[source, 5, e]
        turn = off_s[source, 6, e]
        kept = ((lane - turn) & 127) < 8
        for section, plane in planes:
            for p in range(2):
                quarter = [
                    [pot_v[zt, plane + p, yt] for zt in z_tiles] for yt in y_tiles
                ]
                upper, lower = [jnp.where(lane >= turn, a, b) for a, b in quarter]
                window = jnp.where(jnp.logical_and(line >= drop, kept), upper, 0.0)
                window = jnp.where(jnp.logical_and(line < drop, kept), lower, window)
                start = pl.multiple_of(e * 16 + p * 8, 8)
                windows[section, pl.ds(start, 8), :] = window

    def cut_own(e, carry):
        for n in range(4):
            cut(0, e * 4 + n, ((0, 0), (1, 2)))
        return carry

    def cut_others(e, carry):
        for n in range(4):
            cut(1, e * 4 + n, ((2, 2),))
            cut(2, e * 4 + n, ((3, 0),))
        return carry

    pl.semaphore_wait(barrier, ROWS + COLS)
    off_copies = (
        pltpu.make_async_remote_copy(
            own_off, other_off.at[0], off_send.at[0], off_recv.at[0], below, MESH
        ),
        pltpu.make_async_remote_copy(
            own_off, other_off.at[1], off_send.at[1], off_recv.at[1], above, MESH
        ),
    )
    for copy in off_copies:
        copy.start()

    def tell(k, carry):
        pl.semaphore_signal(
            entered, inc=1, device_id=(row, (col + k) % COLS), device_id_type=MESH
        )
        return carry

    lax.fori_loop(1, COLS, tell, 0)

    def den_copy(slot, half, device):
        part = pl.ds(half * HALF, HALF)
        return pltpu.make_async_remote_copy(
            den_v.at[part, :], near_den.at[slot, part, :],
            den_send.at[slot, half], den_recv.at[slot, half], device, MESH,
        )

    z = row // 2 % 4
    base = row - z * 2
    d_partner = ((row + 8) % ROWS, col)
    den_copies = (
        den_copy(1, 0, d_partner),
        den_copy(2, 0, (base + (z + 1) % 4 * 2, col)),
        den_copy(3, 1, (base + (z + 3) % 4 * 2, col)),
    )
    loads[0].wait()
    pick_rows = (
        lax.broadcasted_iota(I32, (8, NATOMS), 1)
        == row * ATOM_ROWS + lax.broadcasted_iota(I32, (8, NATOMS), 0)
    )
    pick_cols = (
        lax.broadcasted_iota(I32, (NATOMS, TILE_C), 0)
        == col * ATOM_COLS + lax.broadcasted_iota(I32, (NATOMS, TILE_C), 1) // NB
    )
    pick_again = (
        lax.broadcasted_iota(I32, (NATOMS, 128), 0)
        == col * ATOM_COLS + lax.broadcasted_iota(I32, (NATOMS, 128), 1) % ATOM_COLS
    )

    def flags(chosen):
        return jnp.where(chosen, 1.0, 0.0).astype(BF16)

    on_rows = jnp.dot(flags(pick_rows), flags(pattern[...] > 0), preferred_element_type=F32).astype(BF16)
    on_wide = jnp.dot(on_rows, flags(pick_cols), preferred_element_type=F32)
    on_again = jnp.dot(on_rows, flags(pick_again), preferred_element_type=F32)
    mine = (
        lax.broadcasted_iota(I32, (8, 128), 1) // ATOM_COLS == lax.broadcasted_iota(I32, (8, 128), 0)
    )
    info[...] = jnp.zeros((8, 128), I32)
    info[1:2, :] = jnp.sum(
        jnp.where(jnp.logical_and(mine, on_again > 0.0), 1, 0), axis=0, keepdims=True
    )
    for i in range(ATOM_ROWS):
        lines = slice(i * NB, (i + 1) * NB)
        den_v[lines] = jnp.where(on_wide[i : i + 1, :] > 0.0, den_v[lines].astype(F32), 0.0).astype(BF16)
    keep_den = pltpu.make_async_copy(den_v, near_den.at[0], local.at[2])
    keep_den.start()

    for copy in den_copies:
        copy.start()

    own_scalars.wait()
    for copy in pot_loads:
        copy.wait()
    lax.fori_loop(0, ENTRIES // 4, cut_own, 0)

    at = lax.broadcasted_iota(I32, (128, 128), 0)
    to = lax.broadcasted_iota(I32, (128, 128), 1)
    spread = jnp.where(at % 8 == to % 8, 1.0, 0.0).astype(BF16)
    rows = ENTRIES * 16
    at_row = lax.broadcasted_iota(I32, (rows, 128), 0)
    at_lane = lax.broadcasted_iota(I32, (rows, 128), 1)
    right_plane = at_row // 8 % 2 == at_lane // 64
    fold = jnp.where(
        lax.broadcasted_iota(I32, (ENTRIES, rows), 1) // 16
        == lax.broadcasted_iota(I32, (ENTRIES, rows), 0),
        1.0,
        0.0,
    ).astype(BF16)
    unfold = jnp.where(
        lax.broadcasted_iota(I32, (rows, ENTRIES), 0) // 16
        == lax.broadcasted_iota(I32, (rows, ENTRIES), 1),
        1.0,
        0.0,
    ).astype(BF16)
    cell = lax.broadcasted_iota(I32, (ENTRIES, 128), 1) % 8

    def pieces(sections, place_yz):
        drop = upright(place_yz[0:1, :]).astype(F32)
        turn = upright(place_yz[1:2, :])
        drop_rows = jnp.dot(
            unfold, jnp.broadcast_to(drop, (ENTRIES, 128)).astype(BF16), preferred_element_type=F32
        ).astype(I32)
        keep = jnp.logical_and(((at_row - drop_rows) & 7) == at_lane // 8 % 8, right_plane)
        made = []
        for section in sections:
            wide = jnp.dot(windows[section].astype(BF16), spread, preferred_element_type=F32)
            wide = jnp.where(keep, wide, 0.0).astype(BF16)
            piece = jnp.dot(fold, wide, preferred_element_type=F32)
            for s in (1, 2, 4):
                moved = jnp.where(
                    cell + s < 8, pltpu.roll(piece, 128 - s, 1), pltpu.roll(piece, 8 - s, 1)
                )
                piece = jnp.where((turn & s) > 0, moved, piece)
            made.append(piece)
        return made

    for copy in off_copies:
        copy.wait()
    other_scalars = [
        pltpu.make_async_copy(other_off.at[n], off_s.at[n + 1], copy_sem.at[n + 2]) for n in range(2)
    ]
    for copy in other_scalars:
        copy.start()
    table_scalars.wait()

    own_lane = lax.broadcasted_iota(I32, (1, 128), 1) == me

    def write_id(d, carry):
        ids[d] = jnp.where(own_lane, jnp.full((1, 128), table_s[1, d] + 1, I32), 0)
        return carry

    lax.fori_loop(0, DEVICES, write_id, 0)
    for copy in other_scalars:
        copy.wait()
    lax.fori_loop(0, ENTRIES // 4, cut_others, 0)
    to_right[...] = pieces((2,), other_off[0, 5:7, 0:ENTRIES])[0].astype(BF16)
    to_left[...] = pieces((3,), other_off[1, 5:7, 0:ENTRIES])[0].astype(BF16)
    near = (
        pltpu.make_async_remote_copy(to_right, low, near_send.at[0], near_recv.at[0], above, MESH),
        pltpu.make_async_remote_copy(to_left, high, near_send.at[1], near_recv.at[1], below, MESH),
    )
    for copy in near:
        copy.start()
    own_piece = pieces((0, 1), own_off[5:7, 0:ENTRIES])

    def id_copy(target):
        return pltpu.make_async_remote_copy(
            ids.at[target], received_ids.at[me], id_send, id_recv, place_of(target), MESH
        )

    def block_copy(target):
        return pltpu.make_async_remote_copy(
            blocks.at[target], received.at[me], send, recv, place_of(target), MESH
        )

    pl.semaphore_wait(entered, COLS - 1)
    own_id = pltpu.make_async_copy(ids.at[me], received_ids.at[me], local.at[0])
    own_id.start()
    for copy in near:
        copy.wait()
    whole = jnp.concatenate(
        [low[...].astype(F32), own_piece[0], own_piece[1], high[...].astype(F32)], axis=1
    )
    cubes[...] = jnp.where(
        at_x == 0, whole[:, 0:384], jnp.where(at_x == 1, whole[:, 64:448], whole[:, 128:512])
    )
    for copy in loads[1:]:
        copy.wait()

    def make(target):
        e = table_s[0, target]
        weighted = left_v[e] * cubes[pl.ds(e, 1), :].astype(BF16)
        block = lax.dot_general(
            weighted, right_v[e], (((1,), (1,)), ((), ())), preferred_element_type=F32
        )
        blocks[target] = block.astype(BF16)

    def target_at(k):
        return (me + k * STRIDE) % DEVICES

    make(target_at(1))

    def step(k, carry):
        make(target_at(k))
        block_copy(target_at(k - 1)).start()
        id_copy(target_at(k - 1)).start()
        return carry

    lax.fori_loop(2, DEVICES, step, 0)
    block_copy(target_at(DEVICES - 1)).start()
    id_copy(target_at(DEVICES - 1)).start()
    make(me)
    own_block = pltpu.make_async_copy(blocks.at[me], received.at[me], local.at[1])
    own_block.start()
    own_id.wait()
    keep_den.wait()
    own_block.wait()
    all_but_one = pl.ds(0, DEVICES - 1)
    ids_done = pltpu.make_async_remote_copy(
        ids.at[all_but_one], received_ids.at[all_but_one], id_send, id_recv, above, MESH
    )
    blocks_done = pltpu.make_async_remote_copy(
        blocks.at[all_but_one], received.at[all_but_one], send, recv, above, MESH
    )
    ids_done.wait()
    info[0:1, :] = jnp.sum(received_ids[...], axis=0) - 1
    for copy in den_copies:
        copy.wait()
    blocks_done.wait()


def exchange(offsets, pairs, live, pattern, pot, density, left, right):
    dma = pltpu.SemaphoreType.DMA
    return pl.pallas_call(
        exchange_kernel,
        name="exchange",
        out_shape=(
            jax.ShapeDtypeStruct((DEVICES, NB, NB), BF16),
            jax.ShapeDtypeStruct((8, 128), I32),
            jax.ShapeDtypeStruct((4, TILE_R, TILE_C), BF16),
        ),
        in_specs=[far_hbm(), far_hbm(), smem()] + [far_hbm()] * 5,
        out_specs=(hbm(), vmem(), hbm()),
        scratch_shapes=[
            pltpu.VMEM((3, ENTRIES), I32),
            pltpu.VMEM((2, ENTRIES), I32),
            pltpu.VMEM((NATOMS, NATOMS), I32),
            pltpu.VMEM((DEVICES, 1, 128), I32),
            pltpu.VMEM((4, 4, 64, 8, 128), F32),
            pltpu.VMEM((TILE_R, TILE_C), BF16),
            pltpu.VMEM((ENTRIES, NB, CELLS), BF16),
            pltpu.VMEM((ENTRIES, NB, CELLS), BF16),
            pltpu.VMEM((4, ENTRIES * 16, 128), F32),
            pltpu.VMEM((8, 128), I32),
            pltpu.VMEM((2, 8, 128), I32),
            pltpu.SMEM((3, 8, 128), I32),
            pltpu.VMEM((8, 128), I32),
            pltpu.SMEM((8, 128), I32),
            pltpu.VMEM((DEVICES, 1, 128), I32),
            pltpu.VMEM((ENTRIES, 128), BF16),
            pltpu.VMEM((ENTRIES, 128), BF16),
            pltpu.VMEM((ENTRIES, 128), BF16),
            pltpu.VMEM((ENTRIES, 128), BF16),
            pltpu.VMEM((ENTRIES, CELLS), F32),
            pltpu.VMEM((DEVICES, NB, NB), BF16),
            dma((7,)), dma((2,)), dma((2,)), dma((4,)), dma((2,)), dma((2,)),
            dma, dma, dma, dma, dma((4, 2)), dma((4, 2)), dma((3,)),
            dma((3,)), pltpu.SemaphoreType.REGULAR,
        ],
        compiler_params=pltpu.CompilerParams(
            has_side_effects=True, vmem_limit_bytes=48 << 20, collective_id=0
        ),
    )(offsets, pairs, live, pattern, pot, density, left, right)


def combine_kernel(info, received, core, ham, head, after):
    def clear(b, carry):
        head[b] = -1
        return carry

    lax.fori_loop(0, LOCAL, clear, 0)

    def link(s, carry):
        slot = info[0, s]

        @pl.when(slot >= 0)
        def _():
            after[s] = head[slot]
            head[slot] = s

        return carry

    lax.fori_loop(0, DEVICES, link, 0)

    def more(state):
        s, total = state
        return after[s], total + received[s].astype(F32)

    for i in range(ATOM_ROWS):
        for j in range(ATOM_COLS):
            block = i * ATOM_COLS + j
            box = (slice(i * NB, (i + 1) * NB), slice(j * NB, (j + 1) * NB))
            on = info[1, block] > 0

            @pl.when(on)
            def _():
                total = lax.while_loop(
                    lambda state: state[0] >= 0, more, (head[block], core[box].astype(F32))
                )[1]
                ham[box] = total.astype(BF16)

            @pl.when(jnp.logical_not(on))
            def _():
                ham[box] = jnp.zeros((NB, NB), BF16)


def combine(info, received, core):
    return pl.pallas_call(
        combine_kernel,
        name="combine",
        out_shape=jax.ShapeDtypeStruct((TILE_R, TILE_C), BF16),
        in_specs=[smem(), vmem(), vmem()],
        out_specs=vmem(),
        scratch_shapes=[pltpu.SMEM((LOCAL,), I32), pltpu.SMEM((DEVICES,), I32)],
        compiler_params=pltpu.CompilerParams(vmem_limit_bytes=48 << 20),
    )(info, received, core)


def product_kernel(ham, den, out, hbuf, dbuf, load, hsend, dsend, csend, hrecv, drecv):
    row = lax.axis_index("row")
    col = lax.axis_index("col")
    core = row % 2
    z = row // 2 % 4
    ylo = row // 8
    x = col // 2
    yhi = col % 2

    def col_of(x_, h_):
        return x_ % 4 * 2 + h_

    def row_of(l_, z_, c_):
        return l_ * 8 + z_ % 4 * 2 + c_

    def h_at(c, half):
        return hbuf.at[c, pl.ds(half * HALF, HALF), :]

    def d_at(r, half):
        start = pl.multiple_of(r % 2 * TILE_R + half * HALF, HALF)
        return dbuf.at[r // 2, pl.ds(start, HALF), :]

    sent = []

    def h_copy(c, half, target, sem):
        return pltpu.make_async_remote_copy(
            h_at(c, half), h_at(c, half), sem, hrecv.at[c, half], (row, target), MESH
        )

    def d_copy(r, half, target, sem):
        return pltpu.make_async_remote_copy(
            d_at(r, half), d_at(r, half), sem, drecv.at[r, half], (target, col), MESH
        )

    count = {"h": 0, "d": 0, "c": 0}

    def push(kind, make, block, half, target):
        sems = {"h": hsend, "d": dsend, "c": csend}[kind]
        copy = make(block, half, target, sems.at[count[kind]])
        count[kind] += 1
        copy.start()
        sent.append(copy)

    def h_wait(c, half):
        h_copy(c, half, col, hsend.at[0]).wait_recv()

    def d_wait(r, half):
        d_copy(r, half, row, dsend.at[0]).wait_recv()

    other_core = row_of(ylo, z, 1 - core)
    h_partner = col_of(x, 1 - yhi)
    d_partner = row_of(1 - ylo, z, core)
    x_up, x_down = col_of(x + 1, yhi), col_of(x + 3, yhi)
    z_up, z_down = row_of(ylo, z + 1, core), row_of(ylo, z + 3, core)
    h_up, h_down = col_of(x + 1, 1 - yhi), col_of(x + 3, 1 - yhi)
    d_up, d_down = row_of(1 - ylo, z + 1, core), row_of(1 - ylo, z + 3, core)

    first = [pltpu.make_async_copy(ham, hbuf.at[col], load.at[0])] + [
        pltpu.make_async_copy(
            den.at[slot, pl.ds(half * HALF, HALF), :], d_at(r, half), load.at[n + 1]
        )
        for n, (slot, r, half) in enumerate(
            ((0, row, 0), (0, row, 1), (1, d_partner, 0), (2, z_down, 0), (3, z_up, 1))
        )
    ]
    for copy in first:
        copy.start()
    barrier = pltpu.get_barrier_semaphore()
    for peer in (
        (row, x_up), (row, x_down), (row, h_partner),
        (z_up, col), (z_down, col), (d_partner, col), (other_core, col),
    ):
        pl.semaphore_signal(barrier, inc=1, device_id=peer, device_id_type=MESH)
    for copy in first:
        copy.wait()
    pl.semaphore_wait(barrier, 7)

    def share(r, half):
        push("c", d_copy, r, half, other_core)

    def h_both(c):
        for n in range(2):
            h_wait(c, n)

    def d_both(r):
        for n in range(2):
            d_wait(r, n)

    def multiply(k, start, half=None):
        if half is None:
            lines = slice(None)
        else:
            lines = pl.ds(pl.multiple_of(half * HALF, HALF), HALF)

        def tile(n, carry):
            columns = pl.ds(pl.multiple_of(n * 256, 256), 256)
            part = jnp.dot(hbuf[k, lines], dbuf[k, :, columns], preferred_element_type=F32)
            if start:
                out[lines, columns] = part
            else:
                out[lines, columns] += part
            return carry

        lax.fori_loop(0, TILE_C // 256, tile, 0)

    push("d", d_copy, row, 1, d_partner)
    for n in range(2):
        push("h", h_copy, col, n, x_up)
        push("h", h_copy, col, 1 - n, x_down)
        push("h", h_copy, col, n, h_partner)
    push("d", d_copy, row, 1, z_up)
    push("d", d_copy, row, 0, z_down)
    push("d", d_copy, d_partner, 0, z_up)
    push("d", d_copy, z_up, 1, z_down)
    push("d", d_copy, z_down, 0, z_up)
    for r, half in ((row, 0), (row, 1), (d_partner, 0), (z_down, 0), (z_up, 1)):
        share(r, half)

    h_wait(x_down, 0)
    push("h", h_copy, x_down, 0, x_up)
    h_wait(x_up, 1)
    push("h", h_copy, x_up, 1, x_down)
    d_wait(d_partner, 1)
    push("d", d_copy, d_partner, 1, z_down)
    push("d", d_copy, d_partner, 1, z_up)
    push("d", d_copy, d_partner, 0, z_down)
    share(d_partner, 1)
    h_wait(h_partner, 0)
    push("h", h_copy, h_partner, 0, x_up)
    push("h", h_copy, h_partner, 0, x_down)
    d_wait(z_down, 1)
    share(z_down, 1)
    d_wait(z_up, 0)
    share(z_up, 0)
    d_wait(d_down, 0)
    push("d", d_copy, d_down, 0, z_up)
    d_wait(d_up, 1)
    push("d", d_copy, d_up, 1, z_down)
    share(d_down, 0)
    share(d_up, 1)
    h_wait(h_partner, 1)
    push("h", h_copy, h_partner, 1, x_up)
    push("h", h_copy, h_partner, 1, x_down)
    h_wait(x_down, 1)
    h_wait(x_up, 0)
    for n in range(2):
        far = row_of(ylo, z + 2, core)
        d_wait(far, n)
        share(far, n)
    for n in range(2):
        far = col_of(x + 2, yhi)
        h_wait(far, n)
        push("h", h_copy, far, n, h_partner)
    for n in range(4):
        d_both(row_of(ylo, z + n, 1 - core))
    multiply(ylo * 4 + yhi, True)
    multiply(ylo * 4 + 2 + yhi, False)
    d_wait(d_down, 1)
    share(d_down, 1)
    d_wait(d_up, 0)
    share(d_up, 0)
    for n in (0, 1, 3):
        d_both(row_of(1 - ylo, z + n, 1 - core))

    h_far = col_of(x + 2, 1 - yhi)
    late = (1 - ylo) * 4 + (z + 2) % 4
    ready = (1 - ylo) * 4 + yhi
    units = [(k, half) for k in (ready, ready + 2, h_partner) for half in range(2)]
    units += [(k, half) for half in range(2) for k in (h_down, h_up)]
    units += [(h_far, half) for half in range(2)]
    passed = 0
    spots = []
    for k, half in units:
        is_late = jnp.where(k == late, 1, 0)
        spots.append((is_late, len(spots) - passed))
        passed = passed + is_late

    def d_late(n):
        far = row_of(1 - ylo, z + 2, core)
        d_wait(far, n)
        share(far, n)

    for spot in range(len(units) - 2):
        if 6 <= spot + 2:
            h_wait(*units[spot + 2])
        if spot in (6, 7):
            d_late(spot - 6)
        k = 0
        half = 0
        for (unit_k, unit_half), (is_late, at) in zip(units, spots):
            here = jnp.where(at == spot, 1 - is_late, 0)
            k = k + here * unit_k
            half = half + here * unit_half
        multiply(k, False, half)
    d_both(row_of(1 - ylo, z + 2, 1 - core))
    multiply(late, False)
    for copy in sent:
        copy.wait_send()


def multiply_all(ham, den):
    return pl.pallas_call(
        product_kernel,
        name="product",
        out_shape=jax.ShapeDtypeStruct((TILE_R, TILE_C), F32),
        in_specs=[hbm(), hbm()],
        out_specs=vmem(),
        scratch_shapes=[
            pltpu.VMEM((COLS, TILE_R, TILE_C), BF16),
            pltpu.VMEM((COLS, 2 * TILE_R, TILE_C), BF16),
            pltpu.SemaphoreType.DMA((7,)),
            pltpu.SemaphoreType.DMA((16,)),
            pltpu.SemaphoreType.DMA((16,)),
            pltpu.SemaphoreType.DMA((16,)),
            pltpu.SemaphoreType.DMA((COLS, 2)),
            pltpu.SemaphoreType.DMA((ROWS, 2)),
        ],
        compiler_params=pltpu.CompilerParams(
            has_side_effects=True, vmem_limit_bytes=40 << 20, collective_id=1
        ),
    )(ham, den)


def shards(
    potential, basis_left, basis_right, core_matrix, density, pattern, pair_atoms, cube_offsets, live_count
):
    received, info, near_den = exchange(
        cube_offsets.T, pair_atoms.T, live_count, pattern, potential.reshape(4, 64, 8, 512),
        density, basis_left, basis_right,
    )
    ham = combine(info, received, core_matrix)
    return ham, multiply_all(ham, near_den)


def solution(mesh):
    flat = ("row", "col")
    tile = P("row", "col")
    placed = (
        P(flat, None, None),
        P(flat, None, None),
        P(flat, None, None),
        tile,
        tile,
        P(),
        P(flat, None),
        P(flat, None),
        P(flat),
    )
    return jax.shard_map(
        shards, mesh=mesh, in_specs=placed, out_specs=(tile, tile), check_vma=False
    )
```

```python
import functools

import jax
import jax.numpy as jnp
from jax import lax
from jax.experimental import pallas as pl
from jax.experimental.pallas import tpu as pltpu
from jax.sharding import PartitionSpec as P

NATOMS = 64
NB = 128
CELLS = 384
ROWS = 16
COLS = 8
DEVICES = 128
ENTRIES = 64
ATOM_ROWS = 4
ATOM_COLS = 8
LOCAL = ATOM_ROWS * ATOM_COLS
TILE_R = 512
TILE_C = 1024
HALF = 256
STRIDE = 51
PRODUCT_VMEM = 45500000
MESH = pl.DeviceIdType.MESH
F32 = jnp.float32
BF16 = jnp.bfloat16
I32 = jnp.int32


def vmem():
    return pl.BlockSpec(memory_space=pltpu.VMEM)


def smem():
    return pl.BlockSpec(memory_space=pltpu.SMEM)


def hbm():
    return pl.BlockSpec(memory_space=pl.ANY)


def far_hbm():
    return pl.BlockSpec(memory_space=pltpu.HBM)


def place_of(index):
    return (index // COLS, index % COLS)


def exchange_kernel(
    offsets_h, pairs_h, live, pattern_h, pot, density, left, right,
    received, info, near_den,
    offsets, pairs, pattern, received_ids, pot_v, den_v, left_v, right_v, windows, own_off, other_off, off_s, table, table_s, ids,
    to_right, to_left, low, high, cubes, blocks,
    load_sem, off_send, off_recv, copy_sem, near_send, near_recv, send, recv, id_send, id_recv,
    den_send, den_recv, local, small_sem, entered,
):
    row = lax.axis_index("row")
    col = lax.axis_index("col")
    me = row * COLS + col
    above = place_of((me + 1) % DEVICES)
    below = place_of((me + DEVICES - 1) % DEVICES)

    loads = [
        pltpu.make_async_copy(a, b, load_sem.at[n])
        for n, (a, b) in enumerate(((density, den_v), (left, left_v), (right, right_v)))
    ]
    pot_loads = [
        pltpu.make_async_copy(
            pot.at[:, :, :, pl.ds(n * 128, 128)], pot_v.at[n], load_sem.at[n + 3]
        )
        for n in range(4)
    ]
    small = [
        pltpu.make_async_copy(a, b, small_sem.at[n])
        for n, (a, b) in enumerate(((offsets_h, offsets), (pairs_h, pairs), (pattern_h, pattern)))
    ]
    for copy in small + loads[:1] + pot_loads + loads[1:]:
        copy.start()
    barrier = pltpu.get_barrier_semaphore()

    def greet(device):
        pl.semaphore_signal(barrier, inc=1, device_id=device, device_id_type=MESH)

    def greet_row(k, carry):
        greet((row, (col + k) % COLS))
        return carry

    def greet_col(k, carry):
        greet(((row + k) % ROWS, col))
        return carry

    greet(above)
    greet(below)
    lax.fori_loop(1, COLS, greet_row, 0)
    lax.fori_loop(1, ROWS, greet_col, 0)

    for copy in small:
        copy.wait()
    own_off[...] = jnp.zeros((8, 128), I32)
    own_off[0:1, 0:ENTRIES] = offsets[0:1, :]
    own_y = offsets[1:2, :]
    own_z = offsets[2:3, :]
    for n, value in enumerate(
        (
            own_y >> 3,
            jnp.minimum((own_y >> 3) + 1, 63),
            own_z >> 7,
            jnp.minimum((own_z >> 7) + 1, 3),
            own_y & 7,
            own_z & 127,
        )
    ):
        own_off[n + 1 : n + 2, 0:ENTRIES] = value
    own_scalars = pltpu.make_async_copy(own_off, off_s.at[0], copy_sem.at[0])
    own_scalars.start()

    entry = lax.broadcasted_iota(I32, (ENTRIES, ENTRIES), 0)
    eye = entry == lax.broadcasted_iota(I32, (ENTRIES, ENTRIES), 1)

    def upright(line):
        return jnp.sum(jnp.where(eye, line, 0), axis=1, keepdims=True)

    first = pairs[0:1, :]
    second = pairs[1:2, :]
    owner = upright(first // ATOM_ROWS * COLS + second // ATOM_COLS)
    place = upright(first % ATOM_ROWS * ATOM_COLS + second % ATOM_COLS)
    at_x = upright(offsets[0:1, :])
    ordinal = lax.broadcasted_iota(I32, (ENTRIES, DEVICES), 0)
    target_of = lax.broadcasted_iota(I32, (ENTRIES, DEVICES), 1)
    named = jnp.logical_and(owner == target_of, ordinal < live[0])
    table[...] = jnp.zeros((8, 128), I32)
    table[0:1, :] = jnp.sum(jnp.where(named, ordinal, 0), axis=0, keepdims=True)
    table[1:2, :] = jnp.sum(jnp.where(named, place + 1, 0), axis=0, keepdims=True) - 1
    table_scalars = pltpu.make_async_copy(table, table_s, copy_sem.at[1])
    table_scalars.start()

    lane = lax.broadcasted_iota(I32, (8, 128), 1)
    line = lax.broadcasted_iota(I32, (8, 128), 0)

    def cut(source, e, planes):
        y_tiles = (off_s[source, 1, e], off_s[source, 2, e])
        z_tiles = (off_s[source, 3, e], off_s[source, 4, e])
        drop = off_s[source, 5, e]
        turn = off_s[source, 6, e]
        kept = ((lane - turn) & 127) < 8
        for section, plane in planes:
            for p in range(2):
                quarter = [
                    [pot_v[zt, plane + p, yt] for zt in z_tiles] for yt in y_tiles
                ]
                upper, lower = [jnp.where(lane >= turn, a, b) for a, b in quarter]
                window = jnp.where(jnp.logical_and(line >= drop, kept), upper, 0.0)
                window = jnp.where(jnp.logical_and(line < drop, kept), lower, window)
                start = pl.multiple_of(e * 16 + p * 8, 8)
                windows[section, pl.ds(start, 8), :] = window

    def cut_own(e, carry):
        for n in range(4):
            cut(0, e * 4 + n, ((0, 0), (1, 2)))
        return carry

    def cut_others(e, carry):
        for n in range(4):
            cut(1, e * 4 + n, ((2, 2),))
            cut(2, e * 4 + n, ((3, 0),))
        return carry

    pl.semaphore_wait(barrier, ROWS + COLS)
    off_copies = (
        pltpu.make_async_remote_copy(
            own_off, other_off.at[0], off_send.at[0], off_recv.at[0], below, MESH
        ),
        pltpu.make_async_remote_copy(
            own_off, other_off.at[1], off_send.at[1], off_recv.at[1], above, MESH
        ),
    )
    for copy in off_copies:
        copy.start()

    def tell(k, carry):
        pl.semaphore_signal(
            entered, inc=1, device_id=(row, (col + k) % COLS), device_id_type=MESH
        )
        return carry

    lax.fori_loop(1, COLS, tell, 0)

    def den_copy(slot, half, device):
        part = pl.ds(half * HALF, HALF)
        return pltpu.make_async_remote_copy(
            den_v.at[part, :], near_den.at[slot, part, :],
            den_send.at[slot, half], den_recv.at[slot, half], device, MESH,
        )

    z = row // 2 % 4
    base = row - z * 2
    d_partner = ((row + 8) % ROWS, col)
    den_copies = (
        den_copy(1, 0, d_partner),
        den_copy(2, 0, (base + (z + 1) % 4 * 2, col)),
        den_copy(3, 1, (base + (z + 3) % 4 * 2, col)),
    )
    loads[0].wait()
    pick_rows = (
        lax.broadcasted_iota(I32, (8, NATOMS), 1)
        == row * ATOM_ROWS + lax.broadcasted_iota(I32, (8, NATOMS), 0)
    )
    pick_cols = (
        lax.broadcasted_iota(I32, (NATOMS, TILE_C), 0)
        == col * ATOM_COLS + lax.broadcasted_iota(I32, (NATOMS, TILE_C), 1) // NB
    )
    pick_again = (
        lax.broadcasted_iota(I32, (NATOMS, 128), 0)
        == col * ATOM_COLS + lax.broadcasted_iota(I32, (NATOMS, 128), 1) % ATOM_COLS
    )

    def flags(chosen):
        return jnp.where(chosen, 1.0, 0.0).astype(BF16)

    on_rows = jnp.dot(flags(pick_rows), flags(pattern[...] > 0), preferred_element_type=F32).astype(BF16)
    on_wide = jnp.dot(on_rows, flags(pick_cols), preferred_element_type=F32)
    on_again = jnp.dot(on_rows, flags(pick_again), preferred_element_type=F32)
    mine = (
        lax.broadcasted_iota(I32, (8, 128), 1) // ATOM_COLS == lax.broadcasted_iota(I32, (8, 128), 0)
    )
    info[...] = jnp.zeros((8, 128), I32)
    info[1:2, :] = jnp.sum(
        jnp.where(jnp.logical_and(mine, on_again > 0.0), 1, 0), axis=0, keepdims=True
    )
    for i in range(ATOM_ROWS):
        lines = slice(i * NB, (i + 1) * NB)
        den_v[lines] = jnp.where(on_wide[i : i + 1, :] > 0.0, den_v[lines].astype(F32), 0.0).astype(BF16)
    keep_den = pltpu.make_async_copy(den_v, near_den.at[0], local.at[2])
    keep_den.start()

    for copy in den_copies:
        copy.start()

    own_scalars.wait()
    for copy in pot_loads:
        copy.wait()
    lax.fori_loop(0, ENTRIES // 4, cut_own, 0)

    at = lax.broadcasted_iota(I32, (128, 128), 0)
    to = lax.broadcasted_iota(I32, (128, 128), 1)
    spread = jnp.where(at % 8 == to % 8, 1.0, 0.0).astype(BF16)
    rows = ENTRIES * 16
    at_row = lax.broadcasted_iota(I32, (rows, 128), 0)
    at_lane = lax.broadcasted_iota(I32, (rows, 128), 1)
    right_plane = at_row // 8 % 2 == at_lane // 64
    fold = jnp.where(
        lax.broadcasted_iota(I32, (ENTRIES, rows), 1) // 16
        == lax.broadcasted_iota(I32, (ENTRIES, rows), 0),
        1.0,
        0.0,
    ).astype(BF16)
    unfold = jnp.where(
        lax.broadcasted_iota(I32, (rows, ENTRIES), 0) // 16
        == lax.broadcasted_iota(I32, (rows, ENTRIES), 1),
        1.0,
        0.0,
    ).astype(BF16)
    cell = lax.broadcasted_iota(I32, (ENTRIES, 128), 1) % 8

    def pieces(sections, place_yz):
        drop = upright(place_yz[0:1, :]).astype(F32)
        turn = upright(place_yz[1:2, :])
        drop_rows = jnp.dot(
            unfold, jnp.broadcast_to(drop, (ENTRIES, 128)).astype(BF16), preferred_element_type=F32
        ).astype(I32)
        keep = jnp.logical_and(((at_row - drop_rows) & 7) == at_lane // 8 % 8, right_plane)
        made = []
        for section in sections:
            wide = jnp.dot(windows[section].astype(BF16), spread, preferred_element_type=F32)
            wide = jnp.where(keep, wide, 0.0).astype(BF16)
            piece = jnp.dot(fold, wide, preferred_element_type=F32)
            for s in (1, 2, 4):
                moved = jnp.where(
                    cell + s < 8, pltpu.roll(piece, 128 - s, 1), pltpu.roll(piece, 8 - s, 1)
                )
                piece = jnp.where((turn & s) > 0, moved, piece)
            made.append(piece)
        return made

    for copy in off_copies:
        copy.wait()
    other_scalars = [
        pltpu.make_async_copy(other_off.at[n], off_s.at[n + 1], copy_sem.at[n + 2]) for n in range(2)
    ]
    for copy in other_scalars:
        copy.start()
    table_scalars.wait()

    own_lane = lax.broadcasted_iota(I32, (1, 128), 1) == me

    def write_id(d, carry):
        ids[d] = jnp.where(own_lane, jnp.full((1, 128), table_s[1, d] + 1, I32), 0)
        return carry

    lax.fori_loop(0, DEVICES, write_id, 0)
    for copy in other_scalars:
        copy.wait()
    lax.fori_loop(0, ENTRIES // 4, cut_others, 0)
    to_right[...] = pieces((2,), other_off[0, 5:7, 0:ENTRIES])[0].astype(BF16)
    to_left[...] = pieces((3,), other_off[1, 5:7, 0:ENTRIES])[0].astype(BF16)
    near = (
        pltpu.make_async_remote_copy(to_right, low, near_send.at[0], near_recv.at[0], above, MESH),
        pltpu.make_async_remote_copy(to_left, high, near_send.at[1], near_recv.at[1], below, MESH),
    )
    for copy in near:
        copy.start()
    own_piece = pieces((0, 1), own_off[5:7, 0:ENTRIES])

    def id_copy(target):
        return pltpu.make_async_remote_copy(
            ids.at[target], received_ids.at[me], id_send, id_recv, place_of(target), MESH
        )

    def block_copy(target):
        return pltpu.make_async_remote_copy(
            blocks.at[target], received.at[me], send, recv, place_of(target), MESH
        )

    pl.semaphore_wait(entered, COLS - 1)
    own_id = pltpu.make_async_copy(ids.at[me], received_ids.at[me], local.at[0])
    own_id.start()
    for copy in near:
        copy.wait()
    whole = jnp.concatenate(
        [low[...].astype(F32), own_piece[0], own_piece[1], high[...].astype(F32)], axis=1
    )
    cubes[...] = jnp.where(
        at_x == 0, whole[:, 0:384], jnp.where(at_x == 1, whole[:, 64:448], whole[:, 128:512])
    )
    for copy in loads[1:]:
        copy.wait()

    def make(target):
        e = table_s[0, target]
        weighted = left_v[e] * cubes[pl.ds(e, 1), :].astype(BF16)
        block = lax.dot_general(
            weighted, right_v[e], (((1,), (1,)), ((), ())), preferred_element_type=F32
        )
        blocks[target] = block.astype(BF16)

    def target_at(k):
        return (me + k * STRIDE) % DEVICES

    make(target_at(1))

    def step(k, carry):
        make(target_at(k))
        block_copy(target_at(k - 1)).start()
        id_copy(target_at(k - 1)).start()
        return carry

    lax.fori_loop(2, DEVICES, step, 0)
    block_copy(target_at(DEVICES - 1)).start()
    id_copy(target_at(DEVICES - 1)).start()
    make(me)
    own_block = pltpu.make_async_copy(blocks.at[me], received.at[me], local.at[1])
    own_block.start()
    own_id.wait()
    keep_den.wait()
    own_block.wait()
    all_but_one = pl.ds(0, DEVICES - 1)
    ids_done = pltpu.make_async_remote_copy(
        ids.at[all_but_one], received_ids.at[all_but_one], id_send, id_recv, above, MESH
    )
    blocks_done = pltpu.make_async_remote_copy(
        blocks.at[all_but_one], received.at[all_but_one], send, recv, above, MESH
    )
    ids_done.wait()
    info[0:1, :] = jnp.sum(received_ids[...], axis=0) - 1
    for copy in den_copies:
        copy.wait()
    blocks_done.wait()


def exchange(offsets, pairs, live, pattern, pot, density, left, right):
    dma = pltpu.SemaphoreType.DMA
    return pl.pallas_call(
        exchange_kernel,
        name="exchange",
        out_shape=(
            jax.ShapeDtypeStruct((DEVICES, NB, NB), BF16),
            jax.ShapeDtypeStruct((8, 128), I32),
            jax.ShapeDtypeStruct((4, TILE_R, TILE_C), BF16),
        ),
        in_specs=[far_hbm(), far_hbm(), smem()] + [far_hbm()] * 5,
        out_specs=(hbm(), vmem(), hbm()),
        scratch_shapes=[
            pltpu.VMEM((3, ENTRIES), I32),
            pltpu.VMEM((2, ENTRIES), I32),
            pltpu.VMEM((NATOMS, NATOMS), I32),
            pltpu.VMEM((DEVICES, 1, 128), I32),
            pltpu.VMEM((4, 4, 64, 8, 128), F32),
            pltpu.VMEM((TILE_R, TILE_C), BF16),
            pltpu.VMEM((ENTRIES, NB, CELLS), BF16),
            pltpu.VMEM((ENTRIES, NB, CELLS), BF16),
            pltpu.VMEM((4, ENTRIES * 16, 128), F32),
            pltpu.VMEM((8, 128), I32),
            pltpu.VMEM((2, 8, 128), I32),
            pltpu.SMEM((3, 8, 128), I32),
            pltpu.VMEM((8, 128), I32),
            pltpu.SMEM((8, 128), I32),
            pltpu.VMEM((DEVICES, 1, 128), I32),
            pltpu.VMEM((ENTRIES, 128), BF16),
            pltpu.VMEM((ENTRIES, 128), BF16),
            pltpu.VMEM((ENTRIES, 128), BF16),
            pltpu.VMEM((ENTRIES, 128), BF16),
            pltpu.VMEM((ENTRIES, CELLS), F32),
            pltpu.VMEM((DEVICES, NB, NB), BF16),
            dma((7,)), dma((2,)), dma((2,)), dma((4,)), dma((2,)), dma((2,)),
            dma, dma, dma, dma, dma((4, 2)), dma((4, 2)), dma((3,)),
            dma((3,)), pltpu.SemaphoreType.REGULAR,
        ],
        compiler_params=pltpu.CompilerParams(
            has_side_effects=True, vmem_limit_bytes=48 << 20, collective_id=0
        ),
    )(offsets, pairs, live, pattern, pot, density, left, right)


def product_kernel(
    info, received, core_h, den, out, ham,
    hbuf, dbuf, core_v, sums, table, table_s, load, keep_sem, hsend, dsend, csend, hrecv, drecv,
):
    row = lax.axis_index("row")
    col = lax.axis_index("col")
    core = row % 2
    z = row // 2 % 4
    ylo = row // 8
    x = col // 2
    yhi = col % 2

    def col_of(x_, h_):
        return x_ % 4 * 2 + h_

    def row_of(l_, z_, c_):
        return l_ * 8 + z_ % 4 * 2 + c_

    def h_at(c, half):
        return hbuf.at[c, pl.ds(half * HALF, HALF), :]

    def d_at(r, half):
        start = pl.multiple_of(r % 2 * TILE_R + half * HALF, HALF)
        return dbuf.at[r // 2, pl.ds(start, HALF), :]

    sent = []

    def h_copy(c, half, target, sem):
        return pltpu.make_async_remote_copy(
            h_at(c, half), h_at(c, half), sem, hrecv.at[c, half], (row, target), MESH
        )

    def d_copy(r, half, target, sem):
        return pltpu.make_async_remote_copy(
            d_at(r, half), d_at(r, half), sem, drecv.at[r, half], (target, col), MESH
        )

    count = {"h": 0, "d": 0, "c": 0}

    def push(kind, make, block, half, target):
        sems = {"h": hsend, "d": dsend, "c": csend}[kind]
        copy = make(block, half, target, sems.at[count[kind]])
        count[kind] += 1
        copy.start()
        sent.append(copy)

    def h_wait(c, half):
        h_copy(c, half, col, hsend.at[0]).wait_recv()

    def d_wait(r, half):
        d_copy(r, half, row, dsend.at[0]).wait_recv()

    other_core = row_of(ylo, z, 1 - core)
    h_partner = col_of(x, 1 - yhi)
    d_partner = row_of(1 - ylo, z, core)
    x_up, x_down = col_of(x + 1, yhi), col_of(x + 3, yhi)
    z_up, z_down = row_of(ylo, z + 1, core), row_of(ylo, z + 3, core)
    h_up, h_down = col_of(x + 1, 1 - yhi), col_of(x + 3, 1 - yhi)
    d_up, d_down = row_of(1 - ylo, z + 1, core), row_of(1 - ylo, z + 3, core)

    first = [pltpu.make_async_copy(core_h, core_v, load.at[0])] + [
        pltpu.make_async_copy(
            den.at[slot, pl.ds(half * HALF, HALF), :], d_at(r, half), load.at[n + 1]
        )
        for n, (slot, r, half) in enumerate(
            ((0, row, 0), (0, row, 1), (1, d_partner, 0), (2, z_down, 0), (3, z_up, 1))
        )
    ]
    for copy in first:
        copy.start()
    barrier = pltpu.get_barrier_semaphore()
    for peer in (
        (row, x_up), (row, x_down), (row, h_partner),
        (z_up, col), (z_down, col), (d_partner, col), (other_core, col),
    ):
        pl.semaphore_signal(barrier, inc=1, device_id=peer, device_id_type=MESH)
    here = lax.broadcasted_iota(I32, (DEVICES, DEVICES), 0)
    there = lax.broadcasted_iota(I32, (DEVICES, DEVICES), 1)
    slot_row = jnp.where(info[0:1, :] < 0, LOCAL, info[0:1, :])
    slot_col = jnp.sum(jnp.where(here == there, slot_row, 0), axis=1, keepdims=True)
    ahead = jnp.logical_or(
        slot_row < slot_col, jnp.logical_and(slot_row == slot_col, there < here)
    )
    rank = jnp.sum(jnp.where(ahead, 1, 0), axis=1, keepdims=True)
    ranked = rank == there
    in_order = jnp.sum(jnp.where(ranked, slot_col, 0), axis=0, keepdims=True)
    previous = pltpu.roll(jnp.broadcast_to(in_order, (8, DEVICES)), 1, 1)[0:1, :]
    table[...] = jnp.zeros((8, 128), I32)
    table[0:1, :] = jnp.sum(jnp.where(ranked, here, 0), axis=0, keepdims=True)
    table[1:2, :] = jnp.where(
        jnp.logical_and(in_order == previous, there[0:1, :] > 0), 1, 0
    )
    ended = jnp.sum(jnp.where(slot_col <= there, 1, 0), axis=0, keepdims=True)
    table[2:3, :] = jnp.maximum(ended - 1, 0)
    table[3:4, :] = jnp.sum(jnp.where(slot_col == there, 1, 0), axis=0, keepdims=True)
    table[4:5, :] = info[1:2, :]
    scalars = pltpu.make_async_copy(table, table_s, load.at[6])
    scalars.start()
    for copy in first:
        copy.wait()
    pl.semaphore_wait(barrier, 7)

    def share(r, half):
        push("c", d_copy, r, half, other_core)

    def h_both(c):
        for n in range(2):
            h_wait(c, n)

    def d_both(r):
        for n in range(2):
            d_wait(r, n)

    def multiply(k, start, half=None):
        if half is None:
            lines = slice(None)
        else:
            lines = pl.ds(pl.multiple_of(half * HALF, HALF), HALF)

        def tile(n, carry):
            columns = pl.ds(pl.multiple_of(n * 256, 256), 256)
            part = jnp.dot(hbuf[k, lines], dbuf[k, :, columns], preferred_element_type=F32)
            if start:
                out[lines, columns] = part
            else:
                out[lines, columns] += part
            return carry

        lax.fori_loop(0, TILE_C // 256, tile, 0)

    push("d", d_copy, row, 1, d_partner)
    push("d", d_copy, row, 1, z_up)
    push("d", d_copy, row, 0, z_down)
    push("d", d_copy, d_partner, 0, z_up)
    push("d", d_copy, z_up, 1, z_down)
    push("d", d_copy, z_down, 0, z_up)
    for r, half in ((row, 0), (row, 1), (d_partner, 0), (z_down, 0), (z_up, 1)):
        share(r, half)

    scalars.wait()

    def add(p, total):
        same = jnp.full((NB, NB), table_s[1, p], I32) > 0
        total = received[table_s[0, p]].astype(F32) + jnp.where(same, total, 0.0)
        sums[p] = total
        return total

    lax.fori_loop(0, DEVICES, add, jnp.zeros((NB, NB), F32))
    for i in range(ATOM_ROWS):
        for j in range(ATOM_COLS):
            block = i * ATOM_COLS + j
            box = (slice(i * NB, (i + 1) * NB), slice(j * NB, (j + 1) * NB))
            some = jnp.full((NB, NB), table_s[3, block], I32) > 0
            on = jnp.full((NB, NB), table_s[4, block], I32) > 0
            total = core_v[box].astype(F32) + jnp.where(some, sums[table_s[2, block]], 0.0)
            hbuf[col, i * NB : (i + 1) * NB, j * NB : (j + 1) * NB] = jnp.where(on, total, 0.0).astype(BF16)
    keep_ham = pltpu.make_async_copy(hbuf.at[col], ham, keep_sem)
    keep_ham.start()
    for n in range(2):
        push("h", h_copy, col, n, x_up)
        push("h", h_copy, col, 1 - n, x_down)
        push("h", h_copy, col, n, h_partner)

    h_wait(x_down, 0)
    push("h", h_copy, x_down, 0, x_up)
    h_wait(x_up, 1)
    push("h", h_copy, x_up, 1, x_down)
    d_wait(d_partner, 1)
    push("d", d_copy, d_partner, 1, z_down)
    push("d", d_copy, d_partner, 1, z_up)
    push("d", d_copy, d_partner, 0, z_down)
    share(d_partner, 1)
    h_wait(h_partner, 0)
    push("h", h_copy, h_partner, 0, x_up)
    push("h", h_copy, h_partner, 0, x_down)
    d_wait(z_down, 1)
    share(z_down, 1)
    d_wait(z_up, 0)
    share(z_up, 0)
    d_wait(d_down, 0)
    push("d", d_copy, d_down, 0, z_up)
    d_wait(d_up, 1)
    push("d", d_copy, d_up, 1, z_down)
    share(d_down, 0)
    share(d_up, 1)
    h_wait(h_partner, 1)
    push("h", h_copy, h_partner, 1, x_up)
    push("h", h_copy, h_partner, 1, x_down)
    h_wait(x_down, 1)
    h_wait(x_up, 0)
    for n in range(2):
        far = row_of(ylo, z + 2, core)
        d_wait(far, n)
        share(far, n)
    for n in range(2):
        far = col_of(x + 2, yhi)
        h_wait(far, n)
        push("h", h_copy, far, n, h_partner)
    for n in range(4):
        d_both(row_of(ylo, z + n, 1 - core))
    multiply(ylo * 4 + yhi, True)
    multiply(ylo * 4 + 2 + yhi, False)
    d_wait(d_down, 1)
    share(d_down, 1)
    d_wait(d_up, 0)
    share(d_up, 0)
    for n in (0, 1, 3):
        d_both(row_of(1 - ylo, z + n, 1 - core))

    h_far = col_of(x + 2, 1 - yhi)
    late = (1 - ylo) * 4 + (z + 2) % 4
    ready = (1 - ylo) * 4 + yhi
    units = [(k, half) for k in (ready, ready + 2, h_partner) for half in range(2)]
    units += [(k, half) for half in range(2) for k in (h_down, h_up)]
    units += [(h_far, half) for half in range(2)]
    passed = 0
    spots = []
    for k, half in units:
        is_late = jnp.where(k == late, 1, 0)
        spots.append((is_late, len(spots) - passed))
        passed = passed + is_late

    def d_late(n):
        far = row_of(1 - ylo, z + 2, core)
        d_wait(far, n)
        share(far, n)

    for spot in range(len(units) - 2):
        if 6 <= spot + 2:
            h_wait(*units[spot + 2])
        if spot in (6, 7):
            d_late(spot - 6)
        k = 0
        half = 0
        for (unit_k, unit_half), (is_late, at) in zip(units, spots):
            here = jnp.where(at == spot, 1 - is_late, 0)
            k = k + here * unit_k
            half = half + here * unit_half
        multiply(k, False, half)
    d_both(row_of(1 - ylo, z + 2, 1 - core))
    multiply(late, False)
    keep_ham.wait()
    for copy in sent:
        copy.wait_send()


def multiply_all(info, received, core, den):
    dma = pltpu.SemaphoreType.DMA
    return pl.pallas_call(
        product_kernel,
        name="product",
        out_shape=(
            jax.ShapeDtypeStruct((TILE_R, TILE_C), F32),
            jax.ShapeDtypeStruct((TILE_R, TILE_C), BF16),
        ),
        in_specs=[vmem(), vmem(), hbm(), hbm()],
        out_specs=(vmem(), hbm()),
        scratch_shapes=[
            pltpu.VMEM((COLS, TILE_R, TILE_C), BF16),
            pltpu.VMEM((COLS, 2 * TILE_R, TILE_C), BF16),
            pltpu.VMEM((TILE_R, TILE_C), BF16),
            pltpu.VMEM((DEVICES, NB, NB), F32),
            pltpu.VMEM((8, 128), I32),
            pltpu.SMEM((8, 128), I32),
            dma((7,)), dma, dma((16,)), dma((16,)), dma((16,)), dma((COLS, 2)), dma((ROWS, 2)),
        ],
        compiler_params=pltpu.CompilerParams(
            has_side_effects=True, vmem_limit_bytes=PRODUCT_VMEM, collective_id=1
        ),
    )(info, received, core, den)


def shards(
    potential, basis_left, basis_right, core_matrix, density, pattern, pair_atoms, cube_offsets, live_count
):
    received, info, near_den = exchange(
        cube_offsets.T, pair_atoms.T, live_count, pattern, potential.reshape(4, 64, 8, 512),
        density, basis_left, basis_right,
    )
    product, ham = multiply_all(info, received, core_matrix, near_den)
    return ham, product


def solution(mesh):
    flat = ("row", "col")
    tile = P("row", "col")
    placed = (
        P(flat, None, None),
        P(flat, None, None),
        P(flat, None, None),
        tile,
        tile,
        P(),
        P(flat, None),
        P(flat, None),
        P(flat),
    )
    return jax.shard_map(
        shards, mesh=mesh, in_specs=placed, out_specs=(tile, tile), check_vma=False
    )
```

```python
import functools

import jax
import jax.numpy as jnp
from jax import lax
from jax.experimental import pallas as pl
from jax.experimental.pallas import tpu as pltpu
from jax.sharding import PartitionSpec as P

NATOMS = 64
NB = 128
CELLS = 384
ROWS = 16
COLS = 8
DEVICES = 128
ENTRIES = 64
ATOM_ROWS = 4
ATOM_COLS = 8
LOCAL = ATOM_ROWS * ATOM_COLS
TILE_R = 512
TILE_C = 1024
HALF = 256
STRIDE = 51
PRODUCT_VMEM = 45500000
MESH = pl.DeviceIdType.MESH
F32 = jnp.float32
BF16 = jnp.bfloat16
I32 = jnp.int32


def vmem():
    return pl.BlockSpec(memory_space=pltpu.VMEM)


def smem():
    return pl.BlockSpec(memory_space=pltpu.SMEM)


def hbm():
    return pl.BlockSpec(memory_space=pl.ANY)


def far_hbm():
    return pl.BlockSpec(memory_space=pltpu.HBM)


def place_of(index):
    return (index // COLS, index % COLS)


def exchange_kernel(
    offsets_h, pairs_h, live, pattern_h, pot, density, left, right,
    received, info, near_den,
    offsets, pairs, pattern, received_ids, pot_v, den_v, left_v, right_v, windows, own_off, other_off, off_s, table, table_s, ids,
    to_right, to_left, low, high, cubes, blocks,
    load_sem, off_send, off_recv, copy_sem, near_send, near_recv, send, recv, id_send, id_recv,
    den_send, den_recv, local, small_sem, entered,
):
    row = lax.axis_index("row")
    col = lax.axis_index("col")
    me = row * COLS + col
    above = place_of((me + 1) % DEVICES)
    below = place_of((me + DEVICES - 1) % DEVICES)

    loads = [
        pltpu.make_async_copy(a, b, load_sem.at[n])
        for n, (a, b) in enumerate(((density, den_v), (left, left_v), (right, right_v)))
    ]
    pot_loads = [
        pltpu.make_async_copy(
            pot.at[:, :, :, pl.ds(n * 128, 128)], pot_v.at[n], load_sem.at[n + 3]
        )
        for n in range(4)
    ]
    small = [
        pltpu.make_async_copy(a, b, small_sem.at[n])
        for n, (a, b) in enumerate(((offsets_h, offsets), (pairs_h, pairs), (pattern_h, pattern)))
    ]
    for copy in small + loads[:1] + pot_loads + loads[1:]:
        copy.start()
    barrier = pltpu.get_barrier_semaphore()

    def greet(device):
        pl.semaphore_signal(barrier, inc=1, device_id=device, device_id_type=MESH)

    def greet_row(k, carry):
        greet((row, (col + k) % COLS))
        return carry

    def greet_col(k, carry):
        greet(((row + k) % ROWS, col))
        return carry

    greet(above)
    greet(below)
    lax.fori_loop(1, COLS, greet_row, 0)
    lax.fori_loop(1, ROWS, greet_col, 0)

    for copy in small:
        copy.wait()
    own_off[...] = jnp.zeros((8, 128), I32)
    own_off[0:1, 0:ENTRIES] = offsets[0:1, :]
    own_y = offsets[1:2, :]
    own_z = offsets[2:3, :]
    for n, value in enumerate(
        (
            own_y >> 3,
            jnp.minimum((own_y >> 3) + 1, 63),
            own_z >> 7,
            jnp.minimum((own_z >> 7) + 1, 3),
            own_y & 7,
            own_z & 127,
        )
    ):
        own_off[n + 1 : n + 2, 0:ENTRIES] = value
    own_scalars = pltpu.make_async_copy(own_off, off_s.at[0], copy_sem.at[0])
    own_scalars.start()

    entry = lax.broadcasted_iota(I32, (ENTRIES, ENTRIES), 0)
    eye = entry == lax.broadcasted_iota(I32, (ENTRIES, ENTRIES), 1)

    def upright(line):
        return jnp.sum(jnp.where(eye, line, 0), axis=1, keepdims=True)

    first = pairs[0:1, :]
    second = pairs[1:2, :]
    owner = upright(first // ATOM_ROWS * COLS + second // ATOM_COLS)
    place = upright(first % ATOM_ROWS * ATOM_COLS + second % ATOM_COLS)
    at_x = upright(offsets[0:1, :])
    ordinal = lax.broadcasted_iota(I32, (ENTRIES, DEVICES), 0)
    target_of = lax.broadcasted_iota(I32, (ENTRIES, DEVICES), 1)
    named = jnp.logical_and(owner == target_of, ordinal < live[0])
    table[...] = jnp.zeros((8, 128), I32)
    table[0:1, :] = jnp.sum(jnp.where(named, ordinal, 0), axis=0, keepdims=True)
    table[1:2, :] = jnp.sum(jnp.where(named, place + 1, 0), axis=0, keepdims=True) - 1
    table_scalars = pltpu.make_async_copy(table, table_s, copy_sem.at[1])
    table_scalars.start()

    lane = lax.broadcasted_iota(I32, (8, 128), 1)
    line = lax.broadcasted_iota(I32, (8, 128), 0)

    def cut(source, e, planes):
        y_tiles = (off_s[source, 1, e], off_s[source, 2, e])
        z_tiles = (off_s[source, 3, e], off_s[source, 4, e])
        drop = off_s[source, 5, e]
        turn = off_s[source, 6, e]
        kept = ((lane - turn) & 127) < 8
        for section, plane in planes:
            for p in range(2):
                quarter = [
                    [pot_v[zt, plane + p, yt] for zt in z_tiles] for yt in y_tiles
                ]
                upper, lower = [jnp.where(lane >= turn, a, b) for a, b in quarter]
                window = jnp.where(jnp.logical_and(line >= drop, kept), upper, 0.0)
                window = jnp.where(jnp.logical_and(line < drop, kept), lower, window)
                start = pl.multiple_of(e * 16 + p * 8, 8)
                windows[section, pl.ds(start, 8), :] = window

    def cut_own(e, carry):
        for n in range(4):
            cut(0, e * 4 + n, ((0, 0), (1, 2)))
        return carry

    def cut_others(e, carry):
        for n in range(4):
            cut(1, e * 4 + n, ((2, 2),))
            cut(2, e * 4 + n, ((3, 0),))
        return carry

    pl.semaphore_wait(barrier, ROWS + COLS)
    off_copies = (
        pltpu.make_async_remote_copy(
            own_off, other_off.at[0], off_send.at[0], off_recv.at[0], below, MESH
        ),
        pltpu.make_async_remote_copy(
            own_off, other_off.at[1], off_send.at[1], off_recv.at[1], above, MESH
        ),
    )
    for copy in off_copies:
        copy.start()

    def tell(k, carry):
        pl.semaphore_signal(
            entered, inc=1, device_id=(row, (col + k) % COLS), device_id_type=MESH
        )
        return carry

    lax.fori_loop(1, COLS, tell, 0)

    def den_copy(slot, half, device):
        part = pl.ds(half * HALF, HALF)
        return pltpu.make_async_remote_copy(
            den_v.at[part, :], near_den.at[slot, part, :],
            den_send.at[slot, half], den_recv.at[slot, half], device, MESH,
        )

    z = row // 2 % 4
    base = row - z * 2
    d_partner = ((row + 8) % ROWS, col)
    den_copies = (
        den_copy(1, 0, d_partner),
        den_copy(2, 0, (base + (z + 1) % 4 * 2, col)),
        den_copy(3, 1, (base + (z + 3) % 4 * 2, col)),
    )
    loads[0].wait()
    pick_rows = (
        lax.broadcasted_iota(I32, (8, NATOMS), 1)
        == row * ATOM_ROWS + lax.broadcasted_iota(I32, (8, NATOMS), 0)
    )
    pick_cols = (
        lax.broadcasted_iota(I32, (NATOMS, TILE_C), 0)
        == col * ATOM_COLS + lax.broadcasted_iota(I32, (NATOMS, TILE_C), 1) // NB
    )
    pick_again = (
        lax.broadcasted_iota(I32, (NATOMS, 128), 0)
        == col * ATOM_COLS + lax.broadcasted_iota(I32, (NATOMS, 128), 1) % ATOM_COLS
    )

    def flags(chosen):
        return jnp.where(chosen, 1.0, 0.0).astype(BF16)

    on_rows = jnp.dot(flags(pick_rows), flags(pattern[...] > 0), preferred_element_type=F32).astype(BF16)
    on_wide = jnp.dot(on_rows, flags(pick_cols), preferred_element_type=F32)
    on_again = jnp.dot(on_rows, flags(pick_again), preferred_element_type=F32)
    mine = (
        lax.broadcasted_iota(I32, (8, 128), 1) // ATOM_COLS == lax.broadcasted_iota(I32, (8, 128), 0)
    )
    info[...] = jnp.zeros((8, 128), I32)
    info[1:2, :] = jnp.sum(
        jnp.where(jnp.logical_and(mine, on_again > 0.0), 1, 0), axis=0, keepdims=True
    )
    for i in range(ATOM_ROWS):
        lines = slice(i * NB, (i + 1) * NB)
        den_v[lines] = jnp.where(on_wide[i : i + 1, :] > 0.0, den_v[lines].astype(F32), 0.0).astype(BF16)
    keep_den = pltpu.make_async_copy(den_v, near_den.at[0], local.at[2])
    keep_den.start()

    for copy in den_copies:
        copy.start()

    own_scalars.wait()
    for copy in pot_loads:
        copy.wait()
    lax.fori_loop(0, ENTRIES // 4, cut_own, 0)

    at = lax.broadcasted_iota(I32, (128, 128), 0)
    to = lax.broadcasted_iota(I32, (128, 128), 1)
    spread = jnp.where(at % 8 == to % 8, 1.0, 0.0).astype(BF16)
    rows = ENTRIES * 16
    at_row = lax.broadcasted_iota(I32, (rows, 128), 0)
    at_lane = lax.broadcasted_iota(I32, (rows, 128), 1)
    right_plane = at_row // 8 % 2 == at_lane // 64
    fold = jnp.where(
        lax.broadcasted_iota(I32, (ENTRIES, rows), 1) // 16
        == lax.broadcasted_iota(I32, (ENTRIES, rows), 0),
        1.0,
        0.0,
    ).astype(BF16)
    unfold = jnp.where(
        lax.broadcasted_iota(I32, (rows, ENTRIES), 0) // 16
        == lax.broadcasted_iota(I32, (rows, ENTRIES), 1),
        1.0,
        0.0,
    ).astype(BF16)
    cell = lax.broadcasted_iota(I32, (ENTRIES, 128), 1) % 8

    def pieces(sections, place_yz):
        drop = upright(place_yz[0:1, :]).astype(F32)
        turn = upright(place_yz[1:2, :])
        drop_rows = jnp.dot(
            unfold, jnp.broadcast_to(drop, (ENTRIES, 128)).astype(BF16), preferred_element_type=F32
        ).astype(I32)
        keep = jnp.logical_and(((at_row - drop_rows) & 7) == at_lane // 8 % 8, right_plane)
        made = []
        for section in sections:
            wide = jnp.dot(windows[section].astype(BF16), spread, preferred_element_type=F32)
            wide = jnp.where(keep, wide, 0.0).astype(BF16)
            piece = jnp.dot(fold, wide, preferred_element_type=F32)
            for s in (1, 2, 4):
                moved = jnp.where(
                    cell + s < 8, pltpu.roll(piece, 128 - s, 1), pltpu.roll(piece, 8 - s, 1)
                )
                piece = jnp.where((turn & s) > 0, moved, piece)
            made.append(piece)
        return made

    for copy in off_copies:
        copy.wait()
    other_scalars = [
        pltpu.make_async_copy(other_off.at[n], off_s.at[n + 1], copy_sem.at[n + 2]) for n in range(2)
    ]
    for copy in other_scalars:
        copy.start()
    table_scalars.wait()

    own_lane = lax.broadcasted_iota(I32, (1, 128), 1) == me

    def write_id(d, carry):
        ids[d] = jnp.where(own_lane, jnp.full((1, 128), table_s[1, d] + 1, I32), 0)
        return carry

    lax.fori_loop(0, DEVICES, write_id, 0)
    for copy in other_scalars:
        copy.wait()
    lax.fori_loop(0, ENTRIES // 4, cut_others, 0)
    to_right[...] = pieces((2,), other_off[0, 5:7, 0:ENTRIES])[0].astype(BF16)
    to_left[...] = pieces((3,), other_off[1, 5:7, 0:ENTRIES])[0].astype(BF16)
    near = (
        pltpu.make_async_remote_copy(to_right, low, near_send.at[0], near_recv.at[0], above, MESH),
        pltpu.make_async_remote_copy(to_left, high, near_send.at[1], near_recv.at[1], below, MESH),
    )
    for copy in near:
        copy.start()
    own_piece = pieces((0, 1), own_off[5:7, 0:ENTRIES])

    def id_copy(target):
        return pltpu.make_async_remote_copy(
            ids.at[target], received_ids.at[me], id_send, id_recv, place_of(target), MESH
        )

    def block_copy(target):
        return pltpu.make_async_remote_copy(
            blocks.at[target], received.at[me], send, recv, place_of(target), MESH
        )

    pl.semaphore_wait(entered, COLS - 1)
    own_id = pltpu.make_async_copy(ids.at[me], received_ids.at[me], local.at[0])
    own_id.start()
    for copy in near:
        copy.wait()
    whole = jnp.concatenate(
        [low[...].astype(F32), own_piece[0], own_piece[1], high[...].astype(F32)], axis=1
    )
    cubes[...] = jnp.where(
        at_x == 0, whole[:, 0:384], jnp.where(at_x == 1, whole[:, 64:448], whole[:, 128:512])
    )
    for copy in loads[1:]:
        copy.wait()

    def make(target):
        e = table_s[0, target]
        weighted = left_v[e] * cubes[pl.ds(e, 1), :].astype(BF16)
        block = lax.dot_general(
            weighted, right_v[e], (((1,), (1,)), ((), ())), preferred_element_type=F32
        )
        blocks[target] = block.astype(BF16)

    def target_at(k):
        return (me + k * STRIDE) % DEVICES

    make(target_at(1))

    def step(k, carry):
        make(target_at(k))
        block_copy(target_at(k - 1)).start()
        id_copy(target_at(k - 1)).start()
        return carry

    lax.fori_loop(2, DEVICES, step, 0)
    block_copy(target_at(DEVICES - 1)).start()
    id_copy(target_at(DEVICES - 1)).start()
    make(me)
    own_block = pltpu.make_async_copy(blocks.at[me], received.at[me], local.at[1])
    own_block.start()
    own_id.wait()
    keep_den.wait()
    own_block.wait()
    all_but_one = pl.ds(0, DEVICES - 1)
    ids_done = pltpu.make_async_remote_copy(
        ids.at[all_but_one], received_ids.at[all_but_one], id_send, id_recv, above, MESH
    )
    blocks_done = pltpu.make_async_remote_copy(
        blocks.at[all_but_one], received.at[all_but_one], send, recv, above, MESH
    )
    ids_done.wait()
    info[0:1, :] = jnp.sum(received_ids[...], axis=0) - 1
    for copy in den_copies:
        copy.wait()
    blocks_done.wait()


def exchange(offsets, pairs, live, pattern, pot, density, left, right):
    dma = pltpu.SemaphoreType.DMA
    return pl.pallas_call(
        exchange_kernel,
        name="exchange",
        out_shape=(
            jax.ShapeDtypeStruct((DEVICES, NB, NB), BF16),
            jax.ShapeDtypeStruct((8, 128), I32),
            jax.ShapeDtypeStruct((4, TILE_R, TILE_C), BF16),
        ),
        in_specs=[far_hbm(), far_hbm(), smem()] + [far_hbm()] * 5,
        out_specs=(hbm(), vmem(), hbm()),
        scratch_shapes=[
            pltpu.VMEM((3, ENTRIES), I32),
            pltpu.VMEM((2, ENTRIES), I32),
            pltpu.VMEM((NATOMS, NATOMS), I32),
            pltpu.VMEM((DEVICES, 1, 128), I32),
            pltpu.VMEM((4, 4, 64, 8, 128), F32),
            pltpu.VMEM((TILE_R, TILE_C), BF16),
            pltpu.VMEM((ENTRIES, NB, CELLS), BF16),
            pltpu.VMEM((ENTRIES, NB, CELLS), BF16),
            pltpu.VMEM((4, ENTRIES * 16, 128), F32),
            pltpu.VMEM((8, 128), I32),
            pltpu.VMEM((2, 8, 128), I32),
            pltpu.SMEM((3, 8, 128), I32),
            pltpu.VMEM((8, 128), I32),
            pltpu.SMEM((8, 128), I32),
            pltpu.VMEM((DEVICES, 1, 128), I32),
            pltpu.VMEM((ENTRIES, 128), BF16),
            pltpu.VMEM((ENTRIES, 128), BF16),
            pltpu.VMEM((ENTRIES, 128), BF16),
            pltpu.VMEM((ENTRIES, 128), BF16),
            pltpu.VMEM((ENTRIES, CELLS), F32),
            pltpu.VMEM((DEVICES, NB, NB), BF16),
            dma((7,)), dma((2,)), dma((2,)), dma((4,)), dma((2,)), dma((2,)),
            dma, dma, dma, dma, dma((4, 2)), dma((4, 2)), dma((3,)),
            dma((3,)), pltpu.SemaphoreType.REGULAR,
        ],
        compiler_params=pltpu.CompilerParams(
            has_side_effects=True, vmem_limit_bytes=48 << 20, collective_id=0
        ),
    )(offsets, pairs, live, pattern, pot, density, left, right)


def product_kernel(
    info, received, core_h, den, out, ham,
    hbuf, dbuf, core_v, sums, table, table_s, load, keep_sem, hsend, dsend, csend, hrecv, drecv,
):
    row = lax.axis_index("row")
    col = lax.axis_index("col")
    core = row % 2
    z = row // 2 % 4
    ylo = row // 8
    x = col // 2
    yhi = col % 2

    def col_of(x_, h_):
        return x_ % 4 * 2 + h_

    def row_of(l_, z_, c_):
        return l_ * 8 + z_ % 4 * 2 + c_

    def h_at(c, half):
        return hbuf.at[c, pl.ds(half * HALF, HALF), :]

    def d_at(r, half):
        start = pl.multiple_of(r % 2 * TILE_R + half * HALF, HALF)
        return dbuf.at[r // 2, pl.ds(start, HALF), :]

    sent = []

    def h_copy(c, half, target, sem):
        return pltpu.make_async_remote_copy(
            h_at(c, half), h_at(c, half), sem, hrecv.at[c, half], (row, target), MESH
        )

    def d_copy(r, half, target, sem):
        return pltpu.make_async_remote_copy(
            d_at(r, half), d_at(r, half), sem, drecv.at[r, half], (target, col), MESH
        )

    count = {"h": 0, "d": 0, "c": 0}

    def push(kind, make, block, half, target):
        sems = {"h": hsend, "d": dsend, "c": csend}[kind]
        copy = make(block, half, target, sems.at[count[kind]])
        count[kind] += 1
        copy.start()
        sent.append(copy)

    def h_wait(c, half):
        h_copy(c, half, col, hsend.at[0]).wait_recv()

    def d_wait(r, half):
        d_copy(r, half, row, dsend.at[0]).wait_recv()

    other_core = row_of(ylo, z, 1 - core)
    h_partner = col_of(x, 1 - yhi)
    d_partner = row_of(1 - ylo, z, core)
    x_up, x_down = col_of(x + 1, yhi), col_of(x + 3, yhi)
    z_up, z_down = row_of(ylo, z + 1, core), row_of(ylo, z + 3, core)
    h_up, h_down = col_of(x + 1, 1 - yhi), col_of(x + 3, 1 - yhi)
    d_up, d_down = row_of(1 - ylo, z + 1, core), row_of(1 - ylo, z + 3, core)

    first = [pltpu.make_async_copy(core_h, core_v, load.at[0])] + [
        pltpu.make_async_copy(
            den.at[slot, pl.ds(half * HALF, HALF), :], d_at(r, half), load.at[n + 1]
        )
        for n, (slot, r, half) in enumerate(
            ((0, row, 0), (0, row, 1), (1, d_partner, 0), (2, z_down, 0), (3, z_up, 1))
        )
    ]
    for copy in first:
        copy.start()
    barrier = pltpu.get_barrier_semaphore()
    for peer in (
        (row, x_up), (row, x_down), (row, h_partner),
        (z_up, col), (z_down, col), (d_partner, col), (other_core, col),
    ):
        pl.semaphore_signal(barrier, inc=1, device_id=peer, device_id_type=MESH)
    here = lax.broadcasted_iota(I32, (DEVICES, DEVICES), 0)
    there = lax.broadcasted_iota(I32, (DEVICES, DEVICES), 1)
    slot_row = jnp.where(info[0:1, :] < 0, LOCAL, info[0:1, :])
    slot_col = jnp.sum(jnp.where(here == there, slot_row, 0), axis=1, keepdims=True)
    ahead = jnp.logical_or(
        slot_row < slot_col, jnp.logical_and(slot_row == slot_col, there < here)
    )
    rank = jnp.sum(jnp.where(ahead, 1, 0), axis=1, keepdims=True)
    ranked = rank == there
    in_order = jnp.sum(jnp.where(ranked, slot_col, 0), axis=0, keepdims=True)
    previous = pltpu.roll(jnp.broadcast_to(in_order, (8, DEVICES)), 1, 1)[0:1, :]
    table[...] = jnp.zeros((8, 128), I32)
    table[0:1, :] = jnp.sum(jnp.where(ranked, here, 0), axis=0, keepdims=True)
    table[1:2, :] = jnp.where(
        jnp.logical_and(in_order == previous, there[0:1, :] > 0), 1, 0
    )
    ended = jnp.sum(jnp.where(slot_col <= there, 1, 0), axis=0, keepdims=True)
    table[2:3, :] = jnp.maximum(ended - 1, 0)
    table[3:4, :] = jnp.sum(jnp.where(slot_col == there, 1, 0), axis=0, keepdims=True)
    table[4:5, :] = info[1:2, :]
    scalars = pltpu.make_async_copy(table, table_s, load.at[6])
    scalars.start()
    for copy in first:
        copy.wait()
    pl.semaphore_wait(barrier, 7)

    def share(r, half):
        push("c", d_copy, r, half, other_core)

    def h_both(c):
        for n in range(2):
            h_wait(c, n)

    def d_both(r):
        for n in range(2):
            d_wait(r, n)

    def multiply(k, start, half=None):
        if half is None:
            lines = slice(None)
        else:
            lines = pl.ds(pl.multiple_of(half * HALF, HALF), HALF)

        def tile(n, carry):
            columns = pl.ds(pl.multiple_of(n * 512, 512), 512)
            part = jnp.dot(hbuf[k, lines], dbuf[k, :, columns], preferred_element_type=F32)
            if start:
                out[lines, columns] = part
            else:
                out[lines, columns] += part
            return carry

        lax.fori_loop(0, TILE_C // 512, tile, 0)

    push("d", d_copy, row, 1, d_partner)
    push("d", d_copy, row, 1, z_up)
    push("d", d_copy, row, 0, z_down)
    push("d", d_copy, d_partner, 0, z_up)
    push("d", d_copy, z_up, 1, z_down)
    push("d", d_copy, z_down, 0, z_up)
    for r, half in ((row, 0), (row, 1), (d_partner, 0), (z_down, 0), (z_up, 1)):
        share(r, half)

    scalars.wait()

    def add(p, total):
        same = jnp.full((NB, NB), table_s[1, p], I32) > 0
        total = received[table_s[0, p]].astype(F32) + jnp.where(same, total, 0.0)
        sums[p] = total
        return total

    lax.fori_loop(0, DEVICES, add, jnp.zeros((NB, NB), F32), unroll=4)
    for i in range(ATOM_ROWS):
        for j in range(ATOM_COLS):
            block = i * ATOM_COLS + j
            box = (slice(i * NB, (i + 1) * NB), slice(j * NB, (j + 1) * NB))
            some = jnp.full((NB, NB), table_s[3, block], I32) > 0
            on = jnp.full((NB, NB), table_s[4, block], I32) > 0
            total = core_v[box].astype(F32) + jnp.where(some, sums[table_s[2, block]], 0.0)
            hbuf[col, i * NB : (i + 1) * NB, j * NB : (j + 1) * NB] = jnp.where(on, total, 0.0).astype(BF16)
    keep_ham = pltpu.make_async_copy(hbuf.at[col], ham, keep_sem)
    keep_ham.start()
    for n in range(2):
        push("h", h_copy, col, n, x_up)
        push("h", h_copy, col, 1 - n, x_down)
        push("h", h_copy, col, n, h_partner)

    h_wait(x_down, 0)
    push("h", h_copy, x_down, 0, x_up)
    h_wait(x_up, 1)
    push("h", h_copy, x_up, 1, x_down)
    d_wait(d_partner, 1)
    push("d", d_copy, d_partner, 1, z_down)
    push("d", d_copy, d_partner, 1, z_up)
    push("d", d_copy, d_partner, 0, z_down)
    share(d_partner, 1)
    h_wait(h_partner, 0)
    push("h", h_copy, h_partner, 0, x_up)
    push("h", h_copy, h_partner, 0, x_down)
    d_wait(z_down, 1)
    share(z_down, 1)
    d_wait(z_up, 0)
    share(z_up, 0)
    d_wait(d_down, 0)
    push("d", d_copy, d_down, 0, z_up)
    d_wait(d_up, 1)
    push("d", d_copy, d_up, 1, z_down)
    share(d_down, 0)
    share(d_up, 1)
    h_wait(h_partner, 1)
    push("h", h_copy, h_partner, 1, x_up)
    push("h", h_copy, h_partner, 1, x_down)
    h_wait(x_down, 1)
    h_wait(x_up, 0)
    for n in range(2):
        far = row_of(ylo, z + 2, core)
        d_wait(far, n)
        share(far, n)
    for n in range(2):
        far = col_of(x + 2, yhi)
        h_wait(far, n)
        push("h", h_copy, far, n, h_partner)
    for n in range(4):
        d_both(row_of(ylo, z + n, 1 - core))
    multiply(ylo * 4 + yhi, True)
    multiply(ylo * 4 + 2 + yhi, False)
    d_wait(d_down, 1)
    share(d_down, 1)
    d_wait(d_up, 0)
    share(d_up, 0)
    for n in (0, 1, 3):
        d_both(row_of(1 - ylo, z + n, 1 - core))

    h_far = col_of(x + 2, 1 - yhi)
    late = (1 - ylo) * 4 + (z + 2) % 4
    ready = (1 - ylo) * 4 + yhi
    units = [(k, half) for k in (ready, ready + 2, h_partner) for half in range(2)]
    units += [(k, half) for half in range(2) for k in (h_down, h_up)]
    units += [(h_far, half) for half in range(2)]
    passed = 0
    spots = []
    for k, half in units:
        is_late = jnp.where(k == late, 1, 0)
        spots.append((is_late, len(spots) - passed))
        passed = passed + is_late

    def d_late(n):
        far = row_of(1 - ylo, z + 2, core)
        d_wait(far, n)
        share(far, n)

    for spot in range(len(units) - 2):
        if 6 <= spot + 2:
            h_wait(*units[spot + 2])
        if spot in (6, 7):
            d_late(spot - 6)
        k = 0
        half = 0
        for (unit_k, unit_half), (is_late, at) in zip(units, spots):
            here = jnp.where(at == spot, 1 - is_late, 0)
            k = k + here * unit_k
            half = half + here * unit_half
        multiply(k, False, half)
    d_both(row_of(1 - ylo, z + 2, 1 - core))
    multiply(late, False)
    keep_ham.wait()
    for copy in sent:
        copy.wait_send()


def multiply_all(info, received, core, den):
    dma = pltpu.SemaphoreType.DMA
    return pl.pallas_call(
        product_kernel,
        name="product",
        out_shape=(
            jax.ShapeDtypeStruct((TILE_R, TILE_C), F32),
            jax.ShapeDtypeStruct((TILE_R, TILE_C), BF16),
        ),
        in_specs=[vmem(), vmem(), hbm(), hbm()],
        out_specs=(vmem(), hbm()),
        scratch_shapes=[
            pltpu.VMEM((COLS, TILE_R, TILE_C), BF16),
            pltpu.VMEM((COLS, 2 * TILE_R, TILE_C), BF16),
            pltpu.VMEM((TILE_R, TILE_C), BF16),
            pltpu.VMEM((DEVICES, NB, NB), F32),
            pltpu.VMEM((8, 128), I32),
            pltpu.SMEM((8, 128), I32),
            dma((7,)), dma, dma((16,)), dma((16,)), dma((16,)), dma((COLS, 2)), dma((ROWS, 2)),
        ],
        compiler_params=pltpu.CompilerParams(
            has_side_effects=True, vmem_limit_bytes=PRODUCT_VMEM, collective_id=1
        ),
    )(info, received, core, den)


def shards(
    potential, basis_left, basis_right, core_matrix, density, pattern, pair_atoms, cube_offsets, live_count
):
    received, info, near_den = exchange(
        cube_offsets.T, pair_atoms.T, live_count, pattern, potential.reshape(4, 64, 8, 512),
        density, basis_left, basis_right,
    )
    product, ham = multiply_all(info, received, core_matrix, near_den)
    return ham, product


def solution(mesh):
    flat = ("row", "col")
    tile = P("row", "col")
    placed = (
        P(flat, None, None),
        P(flat, None, None),
        P(flat, None, None),
        tile,
        tile,
        P(),
        P(flat, None),
        P(flat, None),
        P(flat),
    )
    return jax.shard_map(
        shards, mesh=mesh, in_specs=placed, out_specs=(tile, tile), check_vma=False
    )
```

```python
import functools

import jax
import jax.numpy as jnp
from jax import lax
from jax.experimental import pallas as pl
from jax.experimental.pallas import tpu as pltpu
from jax.sharding import PartitionSpec as P

NATOMS = 64
NB = 128
CELLS = 384
ROWS = 16
COLS = 8
DEVICES = 128
ENTRIES = 64
ATOM_ROWS = 4
ATOM_COLS = 8
LOCAL = ATOM_ROWS * ATOM_COLS
TILE_R = 512
TILE_C = 1024
HALF = 256
STRIDE = 51
PRODUCT_VMEM = 45500000
MESH = pl.DeviceIdType.MESH
F32 = jnp.float32
BF16 = jnp.bfloat16
I32 = jnp.int32


def vmem():
    return pl.BlockSpec(memory_space=pltpu.VMEM)


def smem():
    return pl.BlockSpec(memory_space=pltpu.SMEM)


def hbm():
    return pl.BlockSpec(memory_space=pl.ANY)


def far_hbm():
    return pl.BlockSpec(memory_space=pltpu.HBM)


def place_of(index):
    return (index // COLS, index % COLS)


def exchange_kernel(
    offsets_h, pairs_h, live, pattern_h, pot, density, left, right,
    received, info, near_den,
    offsets, pairs, pattern, received_ids, pot_v, den_v, left_v, right_v, windows, own_off, other_off, off_s, table, table_s, ids,
    to_right, to_left, low, high, cubes, blocks,
    load_sem, off_send, off_recv, copy_sem, near_send, near_recv, send, recv, id_send, id_recv,
    den_send, den_recv, local, small_sem, entered,
):
    row = lax.axis_index("row")
    col = lax.axis_index("col")
    me = row * COLS + col
    above = place_of((me + 1) % DEVICES)
    below = place_of((me + DEVICES - 1) % DEVICES)

    loads = [
        pltpu.make_async_copy(a, b, load_sem.at[n])
        for n, (a, b) in enumerate(((density, den_v), (left, left_v), (right, right_v)))
    ]
    pot_loads = [
        pltpu.make_async_copy(
            pot.at[:, :, :, pl.ds(n * 128, 128)], pot_v.at[n], load_sem.at[n + 3]
        )
        for n in range(4)
    ]
    small = [
        pltpu.make_async_copy(a, b, small_sem.at[n])
        for n, (a, b) in enumerate(((offsets_h, offsets), (pairs_h, pairs), (pattern_h, pattern)))
    ]
    for copy in small:
        copy.start()
    barrier = pltpu.get_barrier_semaphore()

    def greet(device):
        pl.semaphore_signal(barrier, inc=1, device_id=device, device_id_type=MESH)

    def greet_row(k, carry):
        greet((row, (col + k) % COLS))
        return carry

    def greet_col(k, carry):
        greet(((row + k) % ROWS, col))
        return carry

    greet(above)
    greet(below)
    lax.fori_loop(1, COLS, greet_row, 0)
    lax.fori_loop(1, ROWS, greet_col, 0)

    for copy in loads[:1] + pot_loads + loads[1:]:
        copy.start()
    for copy in small:
        copy.wait()
    own_off[...] = jnp.zeros((8, 128), I32)
    own_off[0:1, 0:ENTRIES] = offsets[0:1, :]
    own_y = offsets[1:2, :]
    own_z = offsets[2:3, :]
    for n, value in enumerate(
        (
            own_y >> 3,
            jnp.minimum((own_y >> 3) + 1, 63),
            own_z >> 7,
            jnp.minimum((own_z >> 7) + 1, 3),
            own_y & 7,
            own_z & 127,
        )
    ):
        own_off[n + 1 : n + 2, 0:ENTRIES] = value
    own_scalars = pltpu.make_async_copy(own_off, off_s.at[0], copy_sem.at[0])
    own_scalars.start()

    entry = lax.broadcasted_iota(I32, (ENTRIES, ENTRIES), 0)
    eye = entry == lax.broadcasted_iota(I32, (ENTRIES, ENTRIES), 1)

    def upright(line):
        return jnp.sum(jnp.where(eye, line, 0), axis=1, keepdims=True)

    first = pairs[0:1, :]
    second = pairs[1:2, :]
    owner = upright(first // ATOM_ROWS * COLS + second // ATOM_COLS)
    place = upright(first % ATOM_ROWS * ATOM_COLS + second % ATOM_COLS)
    at_x = upright(offsets[0:1, :])
    ordinal = lax.broadcasted_iota(I32, (ENTRIES, DEVICES), 0)
    target_of = lax.broadcasted_iota(I32, (ENTRIES, DEVICES), 1)
    named = jnp.logical_and(owner == target_of, ordinal < live[0])
    table[...] = jnp.zeros((8, 128), I32)
    table[0:1, :] = jnp.sum(jnp.where(named, ordinal, 0), axis=0, keepdims=True)
    table[1:2, :] = jnp.sum(jnp.where(named, place + 1, 0), axis=0, keepdims=True) - 1
    table_scalars = pltpu.make_async_copy(table, table_s, copy_sem.at[1])
    table_scalars.start()

    lane = lax.broadcasted_iota(I32, (8, 128), 1)
    line = lax.broadcasted_iota(I32, (8, 128), 0)

    def cut(source, e, planes):
        y_tiles = (off_s[source, 1, e], off_s[source, 2, e])
        z_tiles = (off_s[source, 3, e], off_s[source, 4, e])
        drop = off_s[source, 5, e]
        turn = off_s[source, 6, e]
        kept = ((lane - turn) & 127) < 8
        for section, plane in planes:
            for p in range(2):
                quarter = [
                    [pot_v[zt, plane + p, yt] for zt in z_tiles] for yt in y_tiles
                ]
                upper, lower = [jnp.where(lane >= turn, a, b) for a, b in quarter]
                window = jnp.where(jnp.logical_and(line >= drop, kept), upper, 0.0)
                window = jnp.where(jnp.logical_and(line < drop, kept), lower, window)
                start = pl.multiple_of(e * 16 + p * 8, 8)
                windows[section, pl.ds(start, 8), :] = window

    def cut_own(e, carry):
        for n in range(4):
            cut(0, e * 4 + n, ((0, 0), (1, 2)))
        return carry

    def cut_others(e, carry):
        for n in range(4):
            cut(1, e * 4 + n, ((2, 2),))
            cut(2, e * 4 + n, ((3, 0),))
        return carry

    pl.semaphore_wait(barrier, ROWS + COLS)
    off_copies = (
        pltpu.make_async_remote_copy(
            own_off, other_off.at[0], off_send.at[0], off_recv.at[0], below, MESH
        ),
        pltpu.make_async_remote_copy(
            own_off, other_off.at[1], off_send.at[1], off_recv.at[1], above, MESH
        ),
    )
    for copy in off_copies:
        copy.start()

    def tell(k, carry):
        pl.semaphore_signal(
            entered, inc=1, device_id=(row, (col + k) % COLS), device_id_type=MESH
        )
        return carry

    lax.fori_loop(1, COLS, tell, 0)

    def den_copy(slot, half, device):
        part = pl.ds(half * HALF, HALF)
        return pltpu.make_async_remote_copy(
            den_v.at[part, :], near_den.at[slot, part, :],
            den_send.at[slot, half], den_recv.at[slot, half], device, MESH,
        )

    z = row // 2 % 4
    base = row - z * 2
    d_partner = ((row + 8) % ROWS, col)
    den_copies = (
        den_copy(1, 0, d_partner),
        den_copy(2, 0, (base + (z + 1) % 4 * 2, col)),
        den_copy(3, 1, (base + (z + 3) % 4 * 2, col)),
    )
    loads[0].wait()
    pick_rows = (
        lax.broadcasted_iota(I32, (8, NATOMS), 1)
        == row * ATOM_ROWS + lax.broadcasted_iota(I32, (8, NATOMS), 0)
    )
    pick_cols = (
        lax.broadcasted_iota(I32, (NATOMS, TILE_C), 0)
        == col * ATOM_COLS + lax.broadcasted_iota(I32, (NATOMS, TILE_C), 1) // NB
    )
    pick_again = (
        lax.broadcasted_iota(I32, (NATOMS, 128), 0)
        == col * ATOM_COLS + lax.broadcasted_iota(I32, (NATOMS, 128), 1) % ATOM_COLS
    )

    def flags(chosen):
        return jnp.where(chosen, 1.0, 0.0).astype(BF16)

    on_rows = jnp.dot(flags(pick_rows), flags(pattern[...] > 0), preferred_element_type=F32).astype(BF16)
    on_wide = jnp.dot(on_rows, flags(pick_cols), preferred_element_type=F32)
    on_again = jnp.dot(on_rows, flags(pick_again), preferred_element_type=F32)
    mine = (
        lax.broadcasted_iota(I32, (8, 128), 1) // ATOM_COLS == lax.broadcasted_iota(I32, (8, 128), 0)
    )
    info[...] = jnp.zeros((8, 128), I32)
    info[1:2, :] = jnp.sum(
        jnp.where(jnp.logical_and(mine, on_again > 0.0), 1, 0), axis=0, keepdims=True
    )
    for i in range(ATOM_ROWS):
        lines = slice(i * NB, (i + 1) * NB)
        den_v[lines] = jnp.where(on_wide[i : i + 1, :] > 0.0, den_v[lines].astype(F32), 0.0).astype(BF16)
    keep_den = pltpu.make_async_copy(den_v, near_den.at[0], local.at[2])
    keep_den.start()

    for copy in den_copies:
        copy.start()

    own_scalars.wait()
    for copy in pot_loads:
        copy.wait()
    lax.fori_loop(0, ENTRIES // 4, cut_own, 0)

    at = lax.broadcasted_iota(I32, (128, 128), 0)
    to = lax.broadcasted_iota(I32, (128, 128), 1)
    spread = jnp.where(at % 8 == to % 8, 1.0, 0.0).astype(BF16)
    rows = ENTRIES * 16
    at_row = lax.broadcasted_iota(I32, (rows, 128), 0)
    at_lane = lax.broadcasted_iota(I32, (rows, 128), 1)
    right_plane = at_row // 8 % 2 == at_lane // 64
    fold = jnp.where(
        lax.broadcasted_iota(I32, (ENTRIES, rows), 1) // 16
        == lax.broadcasted_iota(I32, (ENTRIES, rows), 0),
        1.0,
        0.0,
    ).astype(BF16)
    unfold = jnp.where(
        lax.broadcasted_iota(I32, (rows, ENTRIES), 0) // 16
        == lax.broadcasted_iota(I32, (rows, ENTRIES), 1),
        1.0,
        0.0,
    ).astype(BF16)
    cell = lax.broadcasted_iota(I32, (ENTRIES, 128), 1) % 8

    def pieces(sections, place_yz):
        drop = upright(place_yz[0:1, :]).astype(F32)
        turn = upright(place_yz[1:2, :])
        drop_rows = jnp.dot(
            unfold, jnp.broadcast_to(drop, (ENTRIES, 128)).astype(BF16), preferred_element_type=F32
        ).astype(I32)
        keep = jnp.logical_and(((at_row - drop_rows) & 7) == at_lane // 8 % 8, right_plane)
        made = []
        for section in sections:
            wide = jnp.dot(windows[section].astype(BF16), spread, preferred_element_type=F32)
            wide = jnp.where(keep, wide, 0.0).astype(BF16)
            piece = jnp.dot(fold, wide, preferred_element_type=F32)
            for s in (1, 2, 4):
                moved = jnp.where(
                    cell + s < 8, pltpu.roll(piece, 128 - s, 1), pltpu.roll(piece, 8 - s, 1)
                )
                piece = jnp.where((turn & s) > 0, moved, piece)
            made.append(piece)
        return made

    for copy in off_copies:
        copy.wait_recv()
    other_scalars = [
        pltpu.make_async_copy(other_off.at[n], off_s.at[n + 1], copy_sem.at[n + 2]) for n in range(2)
    ]
    for copy in other_scalars:
        copy.start()
    table_scalars.wait()

    own_lane = lax.broadcasted_iota(I32, (1, 128), 1) == me

    def write_id(d, carry):
        ids[d] = jnp.where(own_lane, jnp.full((1, 128), table_s[1, d] + 1, I32), 0)
        return carry

    lax.fori_loop(0, DEVICES, write_id, 0)
    for copy in other_scalars:
        copy.wait()
    lax.fori_loop(0, ENTRIES // 4, cut_others, 0)
    to_right[...] = pieces((2,), other_off[0, 5:7, 0:ENTRIES])[0].astype(BF16)
    to_left[...] = pieces((3,), other_off[1, 5:7, 0:ENTRIES])[0].astype(BF16)
    near = (
        pltpu.make_async_remote_copy(to_right, low, near_send.at[0], near_recv.at[0], above, MESH),
        pltpu.make_async_remote_copy(to_left, high, near_send.at[1], near_recv.at[1], below, MESH),
    )
    for copy in near:
        copy.start()
    own_piece = pieces((0, 1), own_off[5:7, 0:ENTRIES])

    def id_copy(target):
        return pltpu.make_async_remote_copy(
            ids.at[target], received_ids.at[me], id_send, id_recv, place_of(target), MESH
        )

    def block_copy(target):
        return pltpu.make_async_remote_copy(
            blocks.at[target], received.at[me], send, recv, place_of(target), MESH
        )

    pl.semaphore_wait(entered, COLS - 1)
    own_id = pltpu.make_async_copy(ids.at[me], received_ids.at[me], local.at[0])
    own_id.start()
    for copy in near:
        copy.wait_recv()
    whole = jnp.concatenate(
        [low[...].astype(F32), own_piece[0], own_piece[1], high[...].astype(F32)], axis=1
    )
    cubes[...] = jnp.where(
        at_x == 0, whole[:, 0:384], jnp.where(at_x == 1, whole[:, 64:448], whole[:, 128:512])
    )
    for copy in loads[1:]:
        copy.wait()

    def make(target):
        e = table_s[0, target]
        weighted = left_v[e] * cubes[pl.ds(e, 1), :].astype(BF16)
        block = lax.dot_general(
            weighted, right_v[e], (((1,), (1,)), ((), ())), preferred_element_type=F32
        )
        blocks[target] = block.astype(BF16)

    def target_at(k):
        return (me + k * STRIDE) % DEVICES

    make(target_at(1))

    def step(k, carry):
        make(target_at(k))
        block_copy(target_at(k - 1)).start()
        id_copy(target_at(k - 1)).start()
        return carry

    lax.fori_loop(2, DEVICES, step, 0)
    block_copy(target_at(DEVICES - 1)).start()
    id_copy(target_at(DEVICES - 1)).start()
    make(me)
    own_block = pltpu.make_async_copy(blocks.at[me], received.at[me], local.at[1])
    own_block.start()
    own_id.wait()
    keep_den.wait()
    for copy in near + off_copies:
        copy.wait_send()
    own_block.wait()
    all_but_one = pl.ds(0, DEVICES - 1)
    ids_done = pltpu.make_async_remote_copy(
        ids.at[all_but_one], received_ids.at[all_but_one], id_send, id_recv, above, MESH
    )
    blocks_done = pltpu.make_async_remote_copy(
        blocks.at[all_but_one], received.at[all_but_one], send, recv, above, MESH
    )
    ids_done.wait()
    info[0:1, :] = jnp.sum(received_ids[...], axis=0) - 1
    for copy in den_copies:
        copy.wait()
    blocks_done.wait()


def exchange(offsets, pairs, live, pattern, pot, density, left, right):
    dma = pltpu.SemaphoreType.DMA
    return pl.pallas_call(
        exchange_kernel,
        name="exchange",
        out_shape=(
            jax.ShapeDtypeStruct((DEVICES, NB, NB), BF16),
            jax.ShapeDtypeStruct((8, 128), I32),
            jax.ShapeDtypeStruct((4, TILE_R, TILE_C), BF16),
        ),
        in_specs=[far_hbm(), far_hbm(), smem()] + [far_hbm()] * 5,
        out_specs=(hbm(), vmem(), hbm()),
        scratch_shapes=[
            pltpu.VMEM((3, ENTRIES), I32),
            pltpu.VMEM((2, ENTRIES), I32),
            pltpu.VMEM((NATOMS, NATOMS), I32),
            pltpu.VMEM((DEVICES, 1, 128), I32),
            pltpu.VMEM((4, 4, 64, 8, 128), F32),
            pltpu.VMEM((TILE_R, TILE_C), BF16),
            pltpu.VMEM((ENTRIES, NB, CELLS), BF16),
            pltpu.VMEM((ENTRIES, NB, CELLS), BF16),
            pltpu.VMEM((4, ENTRIES * 16, 128), F32),
            pltpu.VMEM((8, 128), I32),
            pltpu.VMEM((2, 8, 128), I32),
            pltpu.SMEM((3, 8, 128), I32),
            pltpu.VMEM((8, 128), I32),
            pltpu.SMEM((8, 128), I32),
            pltpu.VMEM((DEVICES, 1, 128), I32),
            pltpu.VMEM((ENTRIES, 128), BF16),
            pltpu.VMEM((ENTRIES, 128), BF16),
            pltpu.VMEM((ENTRIES, 128), BF16),
            pltpu.VMEM((ENTRIES, 128), BF16),
            pltpu.VMEM((ENTRIES, CELLS), F32),
            pltpu.VMEM((DEVICES, NB, NB), BF16),
            dma((7,)), dma((2,)), dma((2,)), dma((4,)), dma((2,)), dma((2,)),
            dma, dma, dma, dma, dma((4, 2)), dma((4, 2)), dma((3,)),
            dma((3,)), pltpu.SemaphoreType.REGULAR,
        ],
        compiler_params=pltpu.CompilerParams(
            has_side_effects=True, vmem_limit_bytes=48 << 20, collective_id=0
        ),
    )(offsets, pairs, live, pattern, pot, density, left, right)


def product_kernel(
    info, received, core_h, den, out, ham,
    hbuf, dbuf, core_v, sums, table, table_s, load, keep_sem, hsend, dsend, csend, hrecv, drecv,
):
    row = lax.axis_index("row")
    col = lax.axis_index("col")
    core = row % 2
    z = row // 2 % 4
    ylo = row // 8
    x = col // 2
    yhi = col % 2

    def col_of(x_, h_):
        return x_ % 4 * 2 + h_

    def row_of(l_, z_, c_):
        return l_ * 8 + z_ % 4 * 2 + c_

    def h_at(c, half):
        return hbuf.at[c, pl.ds(half * HALF, HALF), :]

    def d_at(r, half):
        start = pl.multiple_of(r % 2 * TILE_R + half * HALF, HALF)
        return dbuf.at[r // 2, pl.ds(start, HALF), :]

    sent = []

    def h_copy(c, half, target, sem):
        return pltpu.make_async_remote_copy(
            h_at(c, half), h_at(c, half), sem, hrecv.at[c, half], (row, target), MESH
        )

    def d_copy(r, half, target, sem):
        return pltpu.make_async_remote_copy(
            d_at(r, half), d_at(r, half), sem, drecv.at[r, half], (target, col), MESH
        )

    count = {"h": 0, "d": 0, "c": 0}

    def push(kind, make, block, half, target):
        sems = {"h": hsend, "d": dsend, "c": csend}[kind]
        copy = make(block, half, target, sems.at[count[kind]])
        count[kind] += 1
        copy.start()
        sent.append(copy)

    def h_wait(c, half):
        h_copy(c, half, col, hsend.at[0]).wait_recv()

    def d_wait(r, half):
        d_copy(r, half, row, dsend.at[0]).wait_recv()

    other_core = row_of(ylo, z, 1 - core)
    h_partner = col_of(x, 1 - yhi)
    d_partner = row_of(1 - ylo, z, core)
    x_up, x_down = col_of(x + 1, yhi), col_of(x + 3, yhi)
    z_up, z_down = row_of(ylo, z + 1, core), row_of(ylo, z + 3, core)
    h_up, h_down = col_of(x + 1, 1 - yhi), col_of(x + 3, 1 - yhi)
    d_up, d_down = row_of(1 - ylo, z + 1, core), row_of(1 - ylo, z + 3, core)

    first = [pltpu.make_async_copy(core_h, core_v, load.at[0])] + [
        pltpu.make_async_copy(
            den.at[slot, pl.ds(half * HALF, HALF), :], d_at(r, half), load.at[n + 1]
        )
        for n, (slot, r, half) in enumerate(
            ((0, row, 0), (0, row, 1), (1, d_partner, 0), (2, z_down, 0), (3, z_up, 1))
        )
    ]
    for copy in first:
        copy.start()
    barrier = pltpu.get_barrier_semaphore()
    for peer in (
        (row, x_up), (row, x_down), (row, h_partner),
        (z_up, col), (z_down, col), (d_partner, col), (other_core, col),
    ):
        pl.semaphore_signal(barrier, inc=1, device_id=peer, device_id_type=MESH)
    here = lax.broadcasted_iota(I32, (DEVICES, DEVICES), 0)
    there = lax.broadcasted_iota(I32, (DEVICES, DEVICES), 1)
    slot_row = jnp.where(info[0:1, :] < 0, LOCAL, info[0:1, :])
    slot_col = jnp.sum(jnp.where(here == there, slot_row, 0), axis=1, keepdims=True)
    ahead = jnp.logical_or(
        slot_row < slot_col, jnp.logical_and(slot_row == slot_col, there < here)
    )
    rank = jnp.sum(jnp.where(ahead, 1, 0), axis=1, keepdims=True)
    ranked = rank == there
    in_order = jnp.sum(jnp.where(ranked, slot_col, 0), axis=0, keepdims=True)
    previous = pltpu.roll(jnp.broadcast_to(in_order, (8, DEVICES)), 1, 1)[0:1, :]
    table[...] = jnp.zeros((8, 128), I32)
    table[0:1, :] = jnp.sum(jnp.where(ranked, here, 0), axis=0, keepdims=True)
    table[1:2, :] = jnp.where(
        jnp.logical_and(in_order == previous, there[0:1, :] > 0), 1, 0
    )
    ended = jnp.sum(jnp.where(slot_col <= there, 1, 0), axis=0, keepdims=True)
    table[2:3, :] = jnp.maximum(ended - 1, 0)
    table[3:4, :] = jnp.sum(jnp.where(slot_col == there, 1, 0), axis=0, keepdims=True)
    table[4:5, :] = info[1:2, :]
    scalars = pltpu.make_async_copy(table, table_s, load.at[6])
    scalars.start()
    for copy in first:
        copy.wait()
    pl.semaphore_wait(barrier, 7)

    def share(r, half):
        push("c", d_copy, r, half, other_core)

    def h_both(c):
        for n in range(2):
            h_wait(c, n)

    def d_both(r):
        for n in range(2):
            d_wait(r, n)

    def multiply(k, start, half=None):
        if half is None:
            lines = slice(None)
        else:
            lines = pl.ds(pl.multiple_of(half * HALF, HALF), HALF)

        def tile(n, carry):
            columns = pl.ds(pl.multiple_of(n * 1024, 1024), 1024)
            part = jnp.dot(hbuf[k, lines], dbuf[k, :, columns], preferred_element_type=F32)
            if start:
                out[lines, columns] = part
            else:
                out[lines, columns] += part
            return carry

        lax.fori_loop(0, TILE_C // 1024, tile, 0)

    push("d", d_copy, row, 1, d_partner)
    push("d", d_copy, row, 1, z_up)
    push("d", d_copy, row, 0, z_down)
    push("d", d_copy, d_partner, 0, z_up)
    push("d", d_copy, z_up, 1, z_down)
    push("d", d_copy, z_down, 0, z_up)
    for r, half in ((row, 0), (row, 1), (d_partner, 0), (z_down, 0), (z_up, 1)):
        share(r, half)

    scalars.wait()

    def add(p, total):
        same = jnp.full((NB, NB), table_s[1, p], I32) > 0
        total = received[table_s[0, p]].astype(F32) + jnp.where(same, total, 0.0)
        sums[p] = total
        return total

    lax.fori_loop(0, DEVICES, add, jnp.zeros((NB, NB), F32), unroll=4)
    for i in range(ATOM_ROWS):
        for j in range(ATOM_COLS):
            block = i * ATOM_COLS + j
            box = (slice(i * NB, (i + 1) * NB), slice(j * NB, (j + 1) * NB))
            some = jnp.full((NB, NB), table_s[3, block], I32) > 0
            on = jnp.full((NB, NB), table_s[4, block], I32) > 0
            total = core_v[box].astype(F32) + jnp.where(some, sums[table_s[2, block]], 0.0)
            hbuf[col, i * NB : (i + 1) * NB, j * NB : (j + 1) * NB] = jnp.where(on, total, 0.0).astype(BF16)
    keep_ham = pltpu.make_async_copy(hbuf.at[col], ham, keep_sem)
    keep_ham.start()
    for n in range(2):
        push("h", h_copy, col, n, x_up)
        push("h", h_copy, col, 1 - n, x_down)
        push("h", h_copy, col, n, h_partner)

    h_wait(x_down, 0)
    push("h", h_copy, x_down, 0, x_up)
    h_wait(x_up, 1)
    push("h", h_copy, x_up, 1, x_down)
    d_wait(d_partner, 1)
    push("d", d_copy, d_partner, 1, z_down)
    push("d", d_copy, d_partner, 1, z_up)
    push("d", d_copy, d_partner, 0, z_down)
    share(d_partner, 1)
    h_wait(h_partner, 0)
    push("h", h_copy, h_partner, 0, x_up)
    push("h", h_copy, h_partner, 0, x_down)
    d_wait(z_down, 1)
    share(z_down, 1)
    d_wait(z_up, 0)
    share(z_up, 0)
    d_wait(d_down, 0)
    push("d", d_copy, d_down, 0, z_up)
    d_wait(d_up, 1)
    push("d", d_copy, d_up, 1, z_down)
    share(d_down, 0)
    share(d_up, 1)
    h_wait(h_partner, 1)
    push("h", h_copy, h_partner, 1, x_up)
    push("h", h_copy, h_partner, 1, x_down)
    h_wait(x_down, 1)
    h_wait(x_up, 0)
    for n in range(2):
        far = row_of(ylo, z + 2, core)
        d_wait(far, n)
        share(far, n)
    for n in range(2):
        far = col_of(x + 2, yhi)
        h_wait(far, n)
        push("h", h_copy, far, n, h_partner)
    for n in range(4):
        d_both(row_of(ylo, z + n, 1 - core))
    multiply(ylo * 4 + yhi, True)
    multiply(ylo * 4 + 2 + yhi, False)
    d_wait(d_down, 1)
    share(d_down, 1)
    d_wait(d_up, 0)
    share(d_up, 0)
    for n in (0, 1, 3):
        d_both(row_of(1 - ylo, z + n, 1 - core))

    h_far = col_of(x + 2, 1 - yhi)
    late = (1 - ylo) * 4 + (z + 2) % 4
    ready = (1 - ylo) * 4 + yhi
    units = [(k, half) for k in (ready, ready + 2, h_partner) for half in range(2)]
    units += [(k, half) for half in range(2) for k in (h_down, h_up)]
    units += [(h_far, half) for half in range(2)]
    passed = 0
    spots = []
    for k, half in units:
        is_late = jnp.where(k == late, 1, 0)
        spots.append((is_late, len(spots) - passed))
        passed = passed + is_late

    def d_late(n):
        far = row_of(1 - ylo, z + 2, core)
        d_wait(far, n)
        share(far, n)

    for spot in range(len(units) - 2):
        if 6 <= spot + 2:
            h_wait(*units[spot + 2])
        if spot in (6, 7):
            d_late(spot - 6)
        k = 0
        half = 0
        for (unit_k, unit_half), (is_late, at) in zip(units, spots):
            here = jnp.where(at == spot, 1 - is_late, 0)
            k = k + here * unit_k
            half = half + here * unit_half
        multiply(k, False, half)
    d_both(row_of(1 - ylo, z + 2, 1 - core))
    multiply(late, False)
    keep_ham.wait()
    for copy in sent:
        copy.wait_send()


def multiply_all(info, received, core, den):
    dma = pltpu.SemaphoreType.DMA
    return pl.pallas_call(
        product_kernel,
        name="product",
        out_shape=(
            jax.ShapeDtypeStruct((TILE_R, TILE_C), F32),
            jax.ShapeDtypeStruct((TILE_R, TILE_C), BF16),
        ),
        in_specs=[vmem(), vmem(), hbm(), hbm()],
        out_specs=(vmem(), hbm()),
        scratch_shapes=[
            pltpu.VMEM((COLS, TILE_R, TILE_C), BF16),
            pltpu.VMEM((COLS, 2 * TILE_R, TILE_C), BF16),
            pltpu.VMEM((TILE_R, TILE_C), BF16),
            pltpu.VMEM((DEVICES, NB, NB), F32),
            pltpu.VMEM((8, 128), I32),
            pltpu.SMEM((8, 128), I32),
            dma((7,)), dma, dma((16,)), dma((16,)), dma((16,)), dma((COLS, 2)), dma((ROWS, 2)),
        ],
        compiler_params=pltpu.CompilerParams(
            has_side_effects=True, vmem_limit_bytes=PRODUCT_VMEM, collective_id=1
        ),
    )(info, received, core, den)


def shards(
    potential, basis_left, basis_right, core_matrix, density, pattern, pair_atoms, cube_offsets, live_count
):
    received, info, near_den = exchange(
        cube_offsets.T, pair_atoms.T, live_count, pattern, potential.reshape(4, 64, 8, 512),
        density, basis_left, basis_right,
    )
    product, ham = multiply_all(info, received, core_matrix, near_den)
    return ham, product


def solution(mesh):
    flat = ("row", "col")
    tile = P("row", "col")
    placed = (
        P(flat, None, None),
        P(flat, None, None),
        P(flat, None, None),
        tile,
        tile,
        P(),
        P(flat, None),
        P(flat, None),
        P(flat),
    )
    return jax.shard_map(
        shards, mesh=mesh, in_specs=placed, out_specs=(tile, tile), check_vma=False
    )
```
